32 devices in a mesh: grp: 2 (over y), seq: 4 (over z), head: 2 (over x), sub: 2 (over core).
Axes of the slice: x: 2, y: 2, z: 4, core: 2. Of those that a mesh axis runs over, the one named last changes fastest.
Arguments:
- queries: float32 [1536, 2048], P(('grp', 'seq'), ('head', 'sub')), parts along dimension 0, may hold values from -6 to 6
- keys: float32 [1536, 2048], P(('grp', 'seq'), ('head', 'sub')), parts along dimension 0, may hold values from -6 to 6
- values: float32 [1536, 2048], P(('grp', 'seq'), ('head', 'sub')), parts along dimension 0, may hold values from -40 to 40
- opt_queries: float32 [16, 64, 2048], P(('grp', 'seq'), None, ('head', 'sub')), parts along dimension 0, may hold values from -6 to 6
- opt_keys: float32 [16, 64, 2048], P(('grp', 'seq'), None, ('head', 'sub')), parts along dimension 0, may hold values from -6 to 6
- opt_values: float32 [16, 64, 2048], P(('grp', 'seq'), None, ('head', 'sub')), parts along dimension 0, may hold values from -40 to 40
- opt_offsets: int32 [16], P(('grp', 'seq')), parts along dimension 0, may hold values from 0 to 192
- opt_lengths: int32 [16], P(('grp', 'seq')), parts along dimension 0, may hold values from 1 to 64, 320 in all
- norm_gain: float32 [2048], P(('head', 'sub')), may hold values from 0.5 to 2
- out_weight: bfloat16 [2048, 4096], P(('head', 'sub')), may hold values from -0.125 to 0.125
Outputs:
- ctx_out: bfloat16 [1536, 4096], P(('grp', 'seq'), ('head', 'sub')), parts along dimension 0
- opt_out: bfloat16 [16, 64, 4096], P(('grp', 'seq'), None, ('head', 'sub')), parts along dimension 0
The draws below stay inside these ranges and needn't reach their ends.
There are 2 independent parts, one for each index of `grp`. The reference program is written for one: setup_inputs(seed, part) draws one part's arguments, and reference() takes and returns one part's arrays. A program takes and returns all parts, laid end to end along the dimension named above; an argument that names none is the same for every part. Nothing has to cross between parts.
Inputs may be any that keep to these rules, and one draw needn't show every extreme that they name: `opt_lengths`: within each scoring group the 8 lengths sum to 320, and the longest option of each group has exactly 64 tokens in every draw.
All inputs are finite; a program needn't handle non-finite values.
Results may differ from the reference program's by a relative error of at most 0.017.
Values may be sent and summed in bfloat16 or wider, within the bound.
A program may use at most 64 MiB of HBM per device.

```python
import math
import jax
import jax.numpy as jnp
import numpy as np
from jax import lax

D = 4096
H = 16
DH = 128
TOK_DEV = 192
OPT_DEV = 2
OPT_LEN = 64
HD = 2048
CONTEXT = 768
OPTS = 8
N_SEQ = 4
N_HEAD = 2
N_SUB = 2


def scaled_values(key, shape):
    base_key, col_key, row_key = jax.random.split(key, 3)
    base = jnp.clip(jax.random.normal(base_key, shape, jnp.float32), -4.0, 4.0)
    col_scale = jnp.exp(jax.random.uniform(col_key, (shape[-1],), jnp.float32, 0.0, math.log(10.0)))
    row_scale = jnp.exp(jax.random.uniform(row_key, shape[:-1] + (1,), jnp.float32, 0.0, math.log(10.0)))
    return 0.1 * base * col_scale * row_scale


def draw_values(key, part):
    return scaled_values(jax.random.fold_in(key, 11), (CONTEXT, HD))


def draw_opt_values(key, part):
    return scaled_values(jax.random.fold_in(key, 23), (OPTS, OPT_LEN, HD))


def set_ends(array, own_key, low, largest):
    spot = [jax.random.randint(jax.random.fold_in(own_key, axis), (), 0, length) for axis, length in enumerate(array.shape)]
    main_axis = array.shape.index(max(array.shape))
    neighbour = spot[:main_axis] + [(spot[main_axis] + 1) % array.shape[main_axis]] + spot[main_axis + 1:]
    return array.at[tuple(spot)].set(low).at[tuple(neighbour)].set(largest)


def block_levels(key, extent, pieces, smallest, high):
    level, own = 1.0, jax.random.fold_in(key, 6)
    for axis_at, parts in pieces:
        heights = jnp.exp(jax.random.uniform(jax.random.fold_in(own, axis_at), (parts,), jnp.float32, smallest / len(pieces), high / len(pieces)))
        level = level * jnp.repeat(heights, extent[axis_at] // parts).reshape([-1 if axis == axis_at else 1 for axis in range(len(extent))])
    return level


def length_profile(amount, total, bound, skew):
    loads = [(1 << 20) // math.isqrt(grade ** skew) + 1 for grade in range(2, amount + 1)]
    rest, counts = total - bound - (amount - 1), [1] * (amount - 1)
    while rest > 0:
        movable = [i for i in range(amount - 1) if counts[i] < bound]
        whole, budget = sum([loads[i] for i in movable]), rest
        for i in movable:
            more = min(bound - counts[i], max(1, budget * loads[i] // whole), rest)
            counts[i] = counts[i] + more
            rest = rest - more
    return np.array([bound] + counts)


def ragged(key, amount, total, most, slope):
    if amount == 2:
        one = jax.random.randint(key, (), max(1, total - most), min(most, total - 1) + 1)
        return jnp.stack([one, total - one])
    tallies = jnp.asarray(length_profile(amount, total, most, slope), jnp.int32)
    twos = (amount - 1) // 2
    donor, taker = tallies[1:1 + 2 * twos:2], tallies[2:2 + 2 * twos:2]
    slack = jnp.minimum(donor - 1, most - taker)
    passed = jax.random.randint(jax.random.fold_in(key, 1), (twos,), 0, 1 << 20) % (slack + 1)
    tallies = tallies.at[1:1 + 2 * twos:2].set(donor - passed).at[2:2 + 2 * twos:2].set(taker + passed)
    return tallies[jax.random.permutation(jax.random.fold_in(key, 2), amount)]


def centred(key, shape, width, bound, pieces=(), kind=jnp.bfloat16):
    level = block_levels(key, shape, pieces, -0.22, 0.18) if pieces else 1.0
    values = jax.random.normal(key, shape, jnp.float32) * width * level
    return jnp.minimum(jnp.maximum(values, -bound), bound).astype(kind)


def setup_inputs(seed: int = 0, part: int = 0) -> dict:
    arg_keys = jax.random.split(jax.random.key(seed), 11)
    part_keys = jax.random.split(jax.random.fold_in(arg_keys[10], part), 11)
    queries = centred(part_keys[0], (CONTEXT, HD), 1.0, 6.0, ((0, 4), (1, 4)), jnp.float32)
    keys = centred(part_keys[1], (CONTEXT, HD), 1.0, 6.0, ((0, 4), (1, 4)), jnp.float32)
    values = draw_values(jax.random.fold_in(jax.random.fold_in(arg_keys[10], part), 71), part)
    opt_queries = centred(part_keys[3], (OPTS, OPT_LEN, HD), 1.0, 6.0, ((0, 4), (2, 4)), jnp.float32)
    opt_keys = centred(part_keys[4], (OPTS, OPT_LEN, HD), 1.0, 6.0, ((0, 4), (2, 4)), jnp.float32)
    opt_values = draw_opt_values(jax.random.fold_in(jax.random.fold_in(arg_keys[10], part), 71), part)
    opt_offsets = set_ends(jax.random.randint(part_keys[6], (OPTS,), 0, TOK_DEV + 1), jax.random.fold_in(part_keys[6], 1), 0, TOK_DEV).astype(jnp.int32)
    opt_lengths = ragged(part_keys[7], OPTS, OPTS * (OPT_LEN * 5 // 8), OPT_LEN, 1).astype(jnp.int32)
    norm_gain = jnp.clip(jnp.exp(math.log(2.0) - 1.3862944 * jax.random.uniform(arg_keys[8], (HD,), jnp.float32) ** block_levels(arg_keys[8], (HD,), ((0, 4),), -0.2, 0.2)), 0.5, 2.0)
    out_weight = centred(arg_keys[9], (HD, D), HD ** -0.5, 0.125, ((0, 4),))
    return {"queries": queries, "keys": keys, "values": values, "opt_queries": opt_queries, "opt_keys": opt_keys, "opt_values": opt_values, "opt_offsets": opt_offsets, "opt_lengths": opt_lengths, "norm_gain": norm_gain, "out_weight": out_weight}


norm_epsilon = 1e-05

def head_norm(attended, gain, mask):
    mean_square = lax.optimization_barrier(jnp.mean(attended * attended, axis=-1, keepdims=True))
    return (attended * lax.rsqrt(mean_square + norm_epsilon) * gain * mask).astype(jnp.bfloat16)

def project_groups(normed, weight_groups):
    groups = weight_groups.shape[0]
    flat = normed.reshape(normed.shape[0], groups, weight_groups.shape[1])
    partial_value = jnp.einsum('rgk,gkd->grd', flat.astype(jnp.float32), weight_groups.astype(jnp.float32), precision=lax.Precision.HIGHEST)
    partial_value = lax.optimization_barrier(partial_value.astype(jnp.bfloat16)).astype(jnp.float32)
    return lax.optimization_barrier(jnp.sum(partial_value, axis=0)).astype(jnp.bfloat16)

def reference(queries, keys, values, opt_queries, opt_keys, opt_values, opt_offsets, opt_lengths, norm_gain, out_weight):
    highest = lax.Precision.HIGHEST
    groups = N_HEAD * N_SUB
    query_blocks = queries.reshape(N_SEQ, TOK_DEV, H, DH)
    key_blocks = keys.reshape(N_SEQ, TOK_DEV, H, DH)
    value_blocks = values.reshape(N_SEQ, TOK_DEV, H, DH)
    states = jnp.einsum('cthd,cthe->chde', key_blocks, value_blocks, precision=highest)
    running = jnp.cumsum(states, axis=0)
    prefix = jnp.concatenate([jnp.zeros((1, H, DH, DH), jnp.float32), running[:-1]], axis=0)
    gain = norm_gain.reshape(H, DH)
    weight_groups = out_weight.reshape(groups, HD // groups, D)
    option_queries = opt_queries.reshape(N_SEQ, OPT_DEV, OPT_LEN, H, DH)
    option_keys = opt_keys.reshape(N_SEQ, OPT_DEV, OPT_LEN, H, DH)
    option_values = opt_values.reshape(N_SEQ, OPT_DEV, OPT_LEN, H, DH)
    offsets = opt_offsets.reshape(N_SEQ, OPT_DEV)
    lengths = opt_lengths.reshape(N_SEQ, OPT_DEV)
    positions = jnp.arange(TOK_DEV, dtype=jnp.int32)
    causal = (positions[:, None] >= positions[None, :]).astype(jnp.float32)
    slots = jnp.arange(OPT_LEN, dtype=jnp.int32)
    slot_causal = (slots[:, None] >= slots[None, :]).astype(jnp.float32)

    def one_block(inputs):
        block_q, block_k, block_v, block_prefix, opt_q, opt_k, opt_v, block_offsets, block_lengths = inputs
        inter = jnp.einsum('thd,hde->the', block_q, block_prefix, precision=highest)
        scores = jnp.einsum('thd,shd->hts', block_q, block_k, precision=highest) * causal[None]
        intra = jnp.einsum('hts,she->the', scores, block_v, precision=highest)
        context_normed = head_norm(inter + intra, gain, 1.0)
        context_rows = project_groups(context_normed.reshape(TOK_DEV, HD), weight_groups)
        before = (positions[None, :] < block_offsets[:, None]).astype(jnp.float32)
        local = jnp.einsum('ot,thd,the->ohde', before, block_k, block_v, precision=highest)
        opt_state = block_prefix[None] + local
        opt_inter = jnp.einsum('oihd,ohde->oihe', opt_q, opt_state, precision=highest)
        opt_scores = jnp.einsum('oihd,ojhd->ohij', opt_q, opt_k, precision=highest) * slot_causal[None, None]
        opt_intra = jnp.einsum('ohij,ojhe->oihe', opt_scores, opt_v, precision=highest)
        valid = (slots[None, :] < block_lengths[:, None]).astype(jnp.float32)
        opt_normed = head_norm(opt_inter + opt_intra, gain, valid[:, :, None, None])
        opt_rows = project_groups(opt_normed.reshape(OPT_DEV * OPT_LEN, HD), weight_groups)
        return (context_rows, opt_rows.reshape(OPT_DEV, OPT_LEN, D))
    context_out, option_out = lax.map(one_block, (query_blocks, key_blocks, value_blocks, prefix, option_queries, option_keys, option_values, offsets, lengths))
    return (context_out.reshape(CONTEXT, D), option_out.reshape(OPTS, OPT_LEN, D))
```

```python
import functools

import jax
import jax.numpy as jnp
from jax import lax
from jax.experimental import pallas as pl
from jax.experimental.pallas import tpu as pltpu
from jax.sharding import PartitionSpec as P

DH = 128
PIECES = 2
PIECE = DH // PIECES
PARTS = 4
END = 384
norm_epsilon = 1e-05
MESH = pl.DeviceIdType.MESH
bf16 = jnp.bfloat16
f32 = jnp.float32


def dot(a, b, ca, cb):
    return lax.dot_general(a, b, (((ca,), (cb,)), ((), ())), preferred_element_type=f32)


def kernel(
    sizes,
    q_hbm, k_hbm, v_hbm, oq_hbm, ok_hbm, ov_hbm, offs_hbm, lens_hbm, gain_hbm, w_hbm,
    ctx_out, opt_out,
    q_buf, k_buf, v_buf, state, intra, pre_recv, pre_send, normed, sib_normed,
    w_own, w_sib, part_send, part_recv, own_part,
    offs, lens, gain_ref,
    in_sem, w_sem, ws_send, ws_recv, pre_ssem, pre_rsem, n_send, n_recv, x_send, x_recv,
):
    n_seq, n_head, n_sub, rows, opts, slots, chunks = sizes
    features = q_hbm.shape[1]
    heads = features // DH
    total = rows + opts * slots
    columns = w_own.shape[2]
    width = columns // chunks
    seq = lax.axis_index("seq")
    head = lax.axis_index("head")
    sub = lax.axis_index("sub")

    barrier = pltpu.get_barrier_semaphore()
    for e in range(1, n_sub):
        pl.semaphore_signal(
            barrier, inc=1, device_id={"sub": lax.rem(sub + e, n_sub)}, device_id_type=MESH
        )
    for d in range(1, n_head):
        pl.semaphore_signal(
            barrier, inc=1, device_id={"head": lax.rem(head + d, n_head)}, device_id_type=MESH
        )

    @pl.when(seq > 0)
    def _():
        pl.semaphore_signal(barrier, inc=1, device_id={"seq": seq - 1}, device_id_type=MESH)

    @pl.when(seq < n_seq - 1)
    def _():
        pl.semaphore_signal(barrier, inc=1, device_id={"seq": seq + 1}, device_id_type=MESH)

    loads = []
    for i, (src, dst, at, count) in enumerate((
        (k_hbm, k_buf, 0, rows),
        (v_hbm, v_buf, 0, rows),
        (q_hbm, q_buf, 0, rows),
        (ok_hbm, k_buf, rows, opts * slots),
        (oq_hbm, q_buf, rows, opts * slots),
        (ov_hbm, v_buf, rows, opts * slots),
    )):
        copy = pltpu.make_async_copy(src, dst.at[pl.ds(at, count)], in_sem.at[i])
        copy.start()
        loads.append(copy)
    for i, (src, dst) in enumerate(((offs_hbm, offs), (lens_hbm, lens), (gain_hbm, gain_ref))):
        copy = pltpu.make_async_copy(src, dst, in_sem.at[6 + i])
        copy.start()
        loads.append(copy)

    def block_of(d, s):
        place = lax.rem(head + d, n_head) * n_sub + s
        return pl.ds(pl.multiple_of(place * columns, columns), columns)

    own_loads = []
    for d in range(n_head):
        copy = pltpu.make_async_copy(w_hbm.at[:, block_of(d, sub)], w_own.at[d], w_sem.at[d])
        own_loads.append(copy)

    def head_cols(h):
        return slice(h * DH, (h + 1) * DH)

    loads[0].wait()
    loads[1].wait()
    for h in range(heads):
        kh = k_buf[:rows, head_cols(h)].astype(bf16)
        vh = v_buf[:rows, head_cols(h)].astype(bf16)
        state[h] = dot(kh, vh, 0, 0)

    @pl.when(seq == 0)
    def _():
        for h in range(heads):
            pre_recv[h] = jnp.zeros((DH, DH), bf16)
            pre_send[h] = state[h].astype(bf16)

    greeted = (n_sub - 1) + (n_head - 1)
    around = jnp.where(seq > 0, 1, 0) + jnp.where(seq < n_seq - 1, 1, 0)
    pl.semaphore_wait(barrier, greeted + around)

    def pre_copy(h, p):
        return pltpu.make_async_remote_copy(
            src_ref=pre_send.at[h, pl.ds(p * PIECE, PIECE)],
            dst_ref=pre_recv.at[h, pl.ds(p * PIECE, PIECE)],
            send_sem=pre_ssem.at[h, p],
            recv_sem=pre_rsem.at[h, p],
            device_id={"seq": seq + 1},
            device_id_type=MESH,
        )

    @pl.when(jnp.logical_and(seq == 0, seq < n_seq - 1))
    def _():
        for h in range(heads):
            for p in range(PIECES):
                pre_copy(h, p).start()

    sib_copies = []
    for d in list(range(1, n_head)) + [0]:
        for e in range(1, n_sub):
            other = lax.rem(sub + e, n_sub)
            copy = pltpu.make_async_remote_copy(
                src_ref=w_hbm.at[:, block_of(d, other)],
                dst_ref=w_sib.at[e - 1, d],
                send_sem=ws_send.at[e - 1, d],
                recv_sem=ws_recv.at[e - 1, d],
                device_id={"sub": other},
                device_id_type=MESH,
            )
            copy.start()
            sib_copies.append(copy)
    for d in list(range(1, n_head)) + [0]:
        own_loads[d].start()

    for i in range(2, 9):
        loads[i].wait()

    ctx_mask = (
        lax.broadcasted_iota(jnp.int32, (rows, rows), 0)
        >= lax.broadcasted_iota(jnp.int32, (rows, rows), 1)
    )
    opt_masks = []
    for o in range(opts):
        col = lax.broadcasted_iota(jnp.int32, (slots, total), 1)
        row = lax.broadcasted_iota(jnp.int32, (slots, total), 0)
        first = rows + o * slots
        here = jnp.logical_and(col >= first, col <= row + first)
        opt_masks.append(jnp.logical_or(col < jnp.minimum(offs[o], rows), here))
    def relay(h):
        for p in range(PIECES):
            pre_copy(h, p).wait_recv()

            @pl.when(seq < n_seq - 1)
            def _():
                at = slice(p * PIECE, (p + 1) * PIECE)
                pre_send[h, at] = (state[h, at] + pre_recv[h, at].astype(f32)).astype(bf16)
                pre_copy(h, p).start()

    for h in range(heads):
        qh = q_buf[:, head_cols(h)].astype(bf16)
        kh = k_buf[:, head_cols(h)].astype(bf16)
        vh = v_buf[:, head_cols(h)].astype(bf16)
        scores = jnp.where(ctx_mask, dot(qh[:rows], kh[:rows], 1, 1), 0.0)
        intra[h, :rows] = dot(scores.astype(bf16), vh[:rows], 1, 0)
        opt_scores = dot(qh[rows:], kh, 1, 1)
        opt_scores = jnp.concatenate([
            jnp.where(opt_masks[o], opt_scores[o * slots:(o + 1) * slots], 0.0)
            for o in range(opts)
        ])
        intra[h, rows:] = dot(opt_scores.astype(bf16), vh, 1, 0)

        @pl.when(seq == 1)
        def _():
            relay(h)

    slot = lax.broadcasted_iota(jnp.int32, (slots, DH), 0)
    valid = [jnp.where(slot < lens[o], 1.0, 0.0) for o in range(opts)]

    n_copies = []
    for h in range(heads):
        @pl.when(seq > 1)
        def _():
            relay(h)

        qh = q_buf[:, head_cols(h)].astype(bf16)
        att = intra[h] + dot(qh, pre_recv[h], 1, 0)
        square = jnp.mean(att * att, axis=-1, keepdims=True)
        out = att * lax.rsqrt(square + norm_epsilon) * gain_ref[:, head_cols(h)]
        normed[:rows, head_cols(h)] = out[:rows].astype(bf16)
        for o in range(opts):
            at = slice(rows + o * slots, rows + (o + 1) * slots)
            normed[at, head_cols(h)] = (out[at] * valid[o]).astype(bf16)
        for e in range(1, n_sub):
            copy = pltpu.make_async_remote_copy(
                src_ref=normed.at[:, pl.ds(h * DH, DH)],
                dst_ref=sib_normed.at[e - 1, :, pl.ds(h * DH, DH)],
                send_sem=n_send.at[e - 1, h],
                recv_sem=n_recv.at[e - 1, h],
                device_id={"sub": lax.rem(sub + e, n_sub)},
                device_id_type=MESH,
            )
            copy.start()
            n_copies.append(copy)

    for d in range(n_head):
        own_loads[d].wait()
    for copy in sib_copies:
        copy.wait_recv()
    for copy in n_copies:
        copy.wait_recv()

    def project(d, c):
        at = pl.ds(c * width, width)
        result = dot(normed[...], w_own[d, :, at], 1, 0)
        for e in range(n_sub - 1):
            result = result + dot(sib_normed[e], w_sib[e, d, :, at], 1, 0)
        return result

    x_copies = {}
    for c in range(chunks):
        for d in range(1, n_head):
            part_send[d - 1, c] = project(d, c).astype(bf16)
            copy = pltpu.make_async_remote_copy(
                src_ref=part_send.at[d - 1, c],
                dst_ref=part_recv.at[d - 1, c],
                send_sem=x_send.at[d - 1, c],
                recv_sem=x_recv.at[d - 1, c],
                device_id={"head": lax.rem(head + d, n_head)},
                device_id_type=MESH,
            )
            copy.start()
            x_copies[d, c] = copy
    for c in range(chunks):
        own_part[c] = project(0, c)
    for c in range(chunks):
        result = own_part[c]
        for d in range(1, n_head):
            x_copies[d, c].wait_recv()
            result = result + part_recv[d - 1, c].astype(f32)
        at = slice(c * width, (c + 1) * width)
        ctx_out[:, at] = result[:rows].astype(bf16)
        opt_out[:, at] = result[rows:].astype(bf16)

    for copy in list(x_copies.values()) + n_copies + sib_copies:
        copy.wait_send()

    @pl.when(seq < n_seq - 1)
    def _():
        for h in range(heads):
            for p in range(PIECES):
                pre_copy(h, p).wait_send()


def shared_kernel(
    sizes,
    q_hbm, k_hbm, v_hbm, oq_hbm, ok_hbm, ov_hbm, offs_hbm, lens_hbm, gain_hbm, w_hbm,
    ctx_out, opt_out,
    q_buf, k_buf, v_buf, state, intra, pre_recv, pre_send, normed, sib_normed, far_normed,
    w_own, w_sib, w_own_end, w_sib_end, w_far, part_send, part_recv, acc,
    offs, lens, gain_ref,
    in_sem, w_sem, ws_send, ws_recv, pre_ssem, pre_rsem, n_send, n_recv,
    f_send, f_recv, r_send, r_recv, x_send, x_recv,
    wx_send, wf_recv, wy_send, wz_send, wd_send,
):
    n_seq, rows, opts, slots, near = sizes
    features = q_hbm.shape[1]
    heads = features // DH
    total = rows + opts * slots
    columns = w_own.shape[1]
    end = columns - near
    parts = w_far.shape[2]
    band = DH // parts
    grp = lax.axis_index("grp")
    seq = lax.axis_index("seq")
    head = lax.axis_index("head")
    sub = lax.axis_index("sub")
    parity = lax.rem(seq, 2)
    mate = seq + 1 - 2 * parity
    sibling = {"sub": 1 - sub}
    across = {"head": 1 - head}
    beside = {"grp": 1 - grp}
    along = {"seq": mate}
    own_q = 2 * grp + parity
    y_q = 2 * (1 - grp) + parity
    z_q = 2 * grp + 1 - parity
    d_q = 2 * (1 - grp) + 1 - parity

    barrier = pltpu.get_barrier_semaphore()
    pl.semaphore_signal(barrier, inc=1, device_id=sibling, device_id_type=MESH)
    pl.semaphore_signal(barrier, inc=1, device_id=beside, device_id_type=MESH)
    for t in range(2):
        pl.semaphore_signal(
            barrier, inc=1, device_id={"head": 1 - head, "sub": t}, device_id_type=MESH
        )

    @pl.when(seq > 0)
    def _():
        pl.semaphore_signal(barrier, inc=1, device_id={"seq": seq - 1}, device_id_type=MESH)

    @pl.when(seq < n_seq - 1)
    def _():
        pl.semaphore_signal(barrier, inc=1, device_id={"seq": seq + 1}, device_id_type=MESH)

    loads = []
    for i, (src, dst, at, count) in enumerate((
        (k_hbm, k_buf, 0, rows),
        (v_hbm, v_buf, 0, rows),
        (q_hbm, q_buf, 0, rows),
        (ok_hbm, k_buf, rows, opts * slots),
        (oq_hbm, q_buf, rows, opts * slots),
        (ov_hbm, v_buf, rows, opts * slots),
    )):
        copy = pltpu.make_async_copy(src, dst.at[pl.ds(at, count)], in_sem.at[i])
        copy.start()
        loads.append(copy)
    for i, (src, dst) in enumerate(((offs_hbm, offs), (lens_hbm, lens), (gain_hbm, gain_ref))):
        copy = pltpu.make_async_copy(src, dst, in_sem.at[6 + i])
        copy.start()
        loads.append(copy)

    def block_of(h, s, start, count):
        return pl.ds(pl.multiple_of((h * 2 + s) * columns + start, 128), count)

    def remote(src, dst, send, recv, where):
        return pltpu.make_async_remote_copy(
            src_ref=src, dst_ref=dst, send_sem=send, recv_sem=recv,
            device_id=where, device_id_type=MESH,
        )

    def head_cols(h):
        return slice(h * DH, (h + 1) * DH)

    around = jnp.where(seq > 0, 1, 0) + jnp.where(seq < n_seq - 1, 1, 0)
    pl.semaphore_wait(barrier, 4 + around)

    wx_copies = []
    for i in range(parts):
        for t in range(2):
            at = pl.ds(pl.multiple_of(own_q * DH + i * band, band), band)
            copy = remote(
                w_hbm.at[at, block_of(1 - head, t, 0, near)], w_far.at[own_q, sub, i],
                wx_send.at[t, i], wf_recv.at[own_q, sub, i], {"head": 1 - head, "sub": t},
            )
            copy.start()
            wx_copies.append(copy)

    def arrived(q, s, i):
        piece = w_far.at[q, s, i]
        remote(piece, piece, wx_send.at[0, 0], wf_recv.at[q, s, i], across).wait_recv()

    def pass_on(q, s, i, send, where):
        piece = w_far.at[q, s, i]
        return remote(piece, piece, send, wf_recv.at[q, s, i], where)

    def y_copy(s, i):
        return pass_on(own_q, s, i, wy_send.at[s, i], beside)

    def z_copy(s, i):
        return pass_on(own_q, s, i, wz_send.at[s, i], along)

    def d_copy(s, i):
        if i % 2 == 0:
            return pass_on(y_q, s, i, wd_send.at[s, i], along)
        return pass_on(z_q, s, i, wd_send.at[s, i], beside)

    def own_event(i):
        for s in range(2):
            arrived(own_q, s, i)
            y_copy(s, i).start()
            z_copy(s, i).start()

    def next_event(i):
        for s in range(2):
            arrived(y_q, s, i)
            if i % 2 == 0:
                d_copy(s, i).start()
        for s in range(2):
            arrived(z_q, s, i)
            if i % 2 == 1:
                d_copy(s, i).start()

    loads[0].wait()
    loads[1].wait()
    for h in range(heads):
        kh = k_buf[:rows, head_cols(h)].astype(bf16)
        vh = v_buf[:rows, head_cols(h)].astype(bf16)
        state[h] = dot(kh, vh, 0, 0)

    def pre_copy(h, p):
        return remote(
            pre_send.at[h, pl.ds(p * PIECE, PIECE)], pre_recv.at[h, pl.ds(p * PIECE, PIECE)],
            pre_ssem.at[h, p], pre_rsem.at[h, p], {"seq": seq + 1},
        )

    @pl.when(seq == 0)
    def _():
        for h in range(heads):
            pre_recv[h] = jnp.zeros((DH, DH), bf16)
            pre_send[h] = state[h].astype(bf16)
        for h in range(heads):
            for p in range(PIECES):
                pre_copy(h, p).start()

    sib_copies = [
        remote(
            w_hbm.at[:, block_of(head, 1 - sub, 0, columns)], w_sib,
            ws_send.at[0], ws_recv.at[0], sibling,
        ),
        remote(
            w_hbm.at[:, block_of(1 - head, 1 - sub, near, end)], w_sib_end,
            ws_send.at[1], ws_recv.at[1], sibling,
        ),
    ]
    own_loads = [
        pltpu.make_async_copy(w_hbm.at[:, block_of(head, sub, 0, columns)], w_own, w_sem.at[0]),
        pltpu.make_async_copy(
            w_hbm.at[:, block_of(1 - head, sub, near, end)], w_own_end, w_sem.at[1]
        ),
    ]
    for copy in sib_copies + own_loads:
        copy.start()

    for i in range(2, 9):
        loads[i].wait()

    ctx_mask = (
        lax.broadcasted_iota(jnp.int32, (rows, rows), 0)
        >= lax.broadcasted_iota(jnp.int32, (rows, rows), 1)
    )
    opt_masks = []
    for o in range(opts):
        col = lax.broadcasted_iota(jnp.int32, (slots, total), 1)
        row = lax.broadcasted_iota(jnp.int32, (slots, total), 0)
        first = rows + o * slots
        here = jnp.logical_and(col >= first, col <= row + first)
        opt_masks.append(jnp.logical_or(col < jnp.minimum(offs[o], rows), here))

    def relay(h):
        for p in range(PIECES):
            pre_copy(h, p).wait_recv()

            @pl.when(seq < n_seq - 1)
            def _():
                at = slice(p * PIECE, (p + 1) * PIECE)
                pre_send[h, at] = (state[h, at] + pre_recv[h, at].astype(f32)).astype(bf16)
                pre_copy(h, p).start()

    for h in range(heads):
        qh = q_buf[:, head_cols(h)].astype(bf16)
        kh = k_buf[:, head_cols(h)].astype(bf16)
        vh = v_buf[:, head_cols(h)].astype(bf16)
        scores = jnp.where(ctx_mask, dot(qh[:rows], kh[:rows], 1, 1), 0.0)
        intra[h, :rows] = dot(scores.astype(bf16), vh[:rows], 1, 0)
        opt_scores = dot(qh[rows:], kh, 1, 1)
        opt_scores = jnp.concatenate([
            jnp.where(opt_masks[o], opt_scores[o * slots:(o + 1) * slots], 0.0)
            for o in range(opts)
        ])
        intra[h, rows:] = dot(opt_scores.astype(bf16), vh, 1, 0)

        @pl.when(seq == 1)
        def _():
            relay(h)

    slot = lax.broadcasted_iota(jnp.int32, (slots, DH), 0)
    valid = [jnp.where(slot < lens[o], 1.0, 0.0) for o in range(opts)]

    @pl.when(seq > 1)
    def _():
        own_event(0)

    n_copies = []
    f_copies = []
    for h in range(heads):
        @pl.when(seq > 1)
        def _():
            relay(h)

        qh = q_buf[:, head_cols(h)].astype(bf16)
        att = intra[h] + dot(qh, pre_recv[h], 1, 0)
        square = jnp.mean(att * att, axis=-1, keepdims=True)
        out = att * lax.rsqrt(square + norm_epsilon) * gain_ref[:, head_cols(h)]
        normed[:rows, head_cols(h)] = out[:rows].astype(bf16)
        for o in range(opts):
            at = slice(rows + o * slots, rows + (o + 1) * slots)
            normed[at, head_cols(h)] = (out[at] * valid[o]).astype(bf16)
        place = pl.ds(pl.multiple_of(sub * DH, DH), DH)
        copy = remote(
            normed.at[:, pl.ds(h * DH, DH)], far_normed.at[h, :, place],
            f_send.at[h], f_recv.at[h], across,
        )
        copy.start()
        f_copies.append(copy)
        copy = remote(
            normed.at[:, pl.ds(h * DH, DH)], sib_normed.at[:, pl.ds(h * DH, DH)],
            n_send.at[h], n_recv.at[h], sibling,
        )
        copy.start()
        n_copies.append(copy)
        if h == 0:
            @pl.when(seq > 2)
            def _():
                own_event(1)

    @pl.when(seq < 2)
    def _():
        own_event(0)

    @pl.when(seq < 3)
    def _():
        own_event(1)

    own_event(2)

    for copy in own_loads:
        copy.wait()
    for copy in sib_copies + n_copies:
        copy.wait_recv()

    result = dot(normed[...], w_own_end[...], 1, 0) + dot(sib_normed[...], w_sib_end[...], 1, 0)
    part_send[...] = result.astype(bf16)
    x_copy = remote(part_send, part_recv, x_send.at[0], x_recv.at[0], across)
    x_copy.start()

    next_event(0)
    step = 256 if columns % 256 == 0 else columns
    for c in range(0, columns, step):
        at = slice(c, c + step)
        acc[:, at] = dot(normed[...], w_own[:, at], 1, 0) + dot(sib_normed[...], w_sib[:, at], 1, 0)
    own_event(3)
    for i in range(4, parts):
        own_event(i)

    r_copies = []

    def hand_over(h):
        f_copies[h].wait_recv()
        piece = far_normed.at[h, :, place]
        copy = remote(piece, piece, r_send.at[h], r_recv.at[h], sibling)
        copy.start()
        r_copies.append(copy)

    for i in range(1, parts - 1):
        next_event(i)
    hand_over(0)
    next_event(parts - 1)
    for h in range(1, heads):
        hand_over(h)
    for i in range(parts):
        for s in range(2):
            arrived(d_q, s, i)
    other = pl.ds(pl.multiple_of((1 - sub) * DH, DH), DH)
    for h in range(heads):
        piece = far_normed.at[h, :, other]
        remote(piece, piece, r_send.at[h], r_recv.at[h], sibling).wait_recv()

    for c in range(0, near, step):
        at = slice(c, min(c + step, near))
        result = acc[:, at]
        for h in range(heads):
            weight = w_far[h, :, :, :, at].reshape(2 * DH, at.stop - at.start)
            result = result + dot(far_normed[h], weight, 1, 0)
        ctx_out[:, at] = result[:rows].astype(bf16)
        opt_out[:, at] = result[rows:].astype(bf16)
    x_copy.wait_recv()
    result = acc[:, near:] + part_recv[...].astype(f32)
    ctx_out[:, near:] = result[:rows].astype(bf16)
    opt_out[:, near:] = result[rows:].astype(bf16)

    for copy in wx_copies + sib_copies + n_copies + f_copies + r_copies + [x_copy]:
        copy.wait_send()
    for s in range(2):
        for i in range(parts):
            y_copy(s, i).wait_send()
            z_copy(s, i).wait_send()
            d_copy(s, i).wait_send()

    @pl.when(seq < n_seq - 1)
    def _():
        for h in range(heads):
            for p in range(PIECES):
                pre_copy(h, p).wait_send()


def shared_call(n_seq, rows, opts, slots, features, columns):
    heads = features // DH
    total = rows + opts * slots
    near = columns - END
    sem = pltpu.SemaphoreType.DMA
    anyspace = pl.BlockSpec(memory_space=pl.ANY)
    vmem = pl.BlockSpec(memory_space=pltpu.VMEM)
    return pl.pallas_call(
        functools.partial(shared_kernel, (n_seq, rows, opts, slots, near)),
        out_shape=(
            pltpu.VMEM((rows, columns), bf16),
            pltpu.VMEM((opts * slots, columns), bf16),
        ),
        in_specs=[anyspace] * 10,
        out_specs=(vmem, vmem),
        scratch_shapes=[
            pltpu.VMEM((total, features), f32),
            pltpu.VMEM((total, features), f32),
            pltpu.VMEM((total, features), f32),
            pltpu.VMEM((heads, DH, DH), f32),
            pltpu.VMEM((heads, total, DH), f32),
            pltpu.VMEM((heads, DH, DH), bf16),
            pltpu.VMEM((heads, DH, DH), bf16),
            pltpu.VMEM((total, features), bf16),
            pltpu.VMEM((total, features), bf16),
            pltpu.VMEM((heads, total, 2 * DH), bf16),
            pltpu.VMEM((features, columns), bf16),
            pltpu.VMEM((features, columns), bf16),
            pltpu.VMEM((features, END), bf16),
            pltpu.VMEM((features, END), bf16),
            pltpu.VMEM((heads, 2, PARTS, DH // PARTS, near), bf16),
            pltpu.VMEM((total, END), bf16),
            pltpu.VMEM((total, END), bf16),
            pltpu.VMEM((total, columns), f32),
            pltpu.SMEM((opts,), jnp.int32),
            pltpu.SMEM((opts,), jnp.int32),
            pltpu.VMEM((1, features), f32),
            sem((9,)),
            sem((2,)),
            sem((2,)),
            sem((2,)),
            sem((heads, PIECES)),
            sem((heads, PIECES)),
            sem((heads,)),
            sem((heads,)),
            sem((heads,)),
            sem((heads,)),
            sem((heads,)),
            sem((heads,)),
            sem((1,)),
            sem((1,)),
            sem((2, PARTS)),
            sem((heads, 2, PARTS)),
            sem((2, PARTS)),
            sem((2, PARTS)),
            sem((2, PARTS)),
        ],
        compiler_params=pltpu.CompilerParams(collective_id=0, has_side_effects=True),
        name="scoring",
    )


def write_out(ctx, opt, ctx_hbm, opt_hbm, out_sem):
    copies = [
        pltpu.make_async_copy(ctx, ctx_hbm, out_sem.at[0]),
        pltpu.make_async_copy(opt, opt_hbm, out_sem.at[1]),
    ]
    for copy in copies:
        copy.start()
    for copy in copies:
        copy.wait()


def on_device(
    queries, keys, values, opt_queries, opt_keys, opt_values,
    opt_offsets, opt_lengths, norm_gain, out_weight,
):
    n_seq, n_head, n_sub = (lax.axis_size(a) for a in ("seq", "head", "sub"))
    rows, features = queries.shape
    opts, slots, _ = opt_queries.shape
    heads = features // DH
    total = rows + opts * slots
    columns = out_weight.shape[1] // (n_head * n_sub)
    width = 256 if columns % 256 == 0 else columns
    chunks = columns // width
    flat = lambda a: a.reshape(opts * slots, features)
    anyspace = pl.BlockSpec(memory_space=pl.ANY)
    vmem = pl.BlockSpec(memory_space=pltpu.VMEM)
    sem = pltpu.SemaphoreType.DMA
    shared = (
        lax.axis_size("grp") == 2 and n_head == 2 and n_sub == 2 and n_seq % 2 == 0
        and heads == 4 and columns > END
    )
    if shared:
        scoring = shared_call(n_seq, rows, opts, slots, features, columns)
    else:
        scoring = pl.pallas_call(
            functools.partial(kernel, (n_seq, n_head, n_sub, rows, opts, slots, chunks)),
            out_shape=(
                pltpu.VMEM((rows, columns), bf16),
                pltpu.VMEM((opts * slots, columns), bf16),
            ),
            in_specs=[anyspace] * 10,
            out_specs=(vmem, vmem),
            scratch_shapes=[
                pltpu.VMEM((total, features), f32),
                pltpu.VMEM((total, features), f32),
                pltpu.VMEM((total, features), f32),
                pltpu.VMEM((heads, DH, DH), f32),
                pltpu.VMEM((heads, total, DH), f32),
                pltpu.VMEM((heads, DH, DH), bf16),
                pltpu.VMEM((heads, DH, DH), bf16),
                pltpu.VMEM((total, features), bf16),
                pltpu.VMEM((n_sub - 1, total, features), bf16),
                pltpu.VMEM((n_head, features, columns), bf16),
                pltpu.VMEM((n_sub - 1, n_head, features, columns), bf16),
                pltpu.VMEM((n_head - 1, chunks, total, width), bf16),
                pltpu.VMEM((n_head - 1, chunks, total, width), bf16),
                pltpu.VMEM((chunks, total, width), f32),
                pltpu.SMEM((opts,), jnp.int32),
                pltpu.SMEM((opts,), jnp.int32),
                pltpu.VMEM((1, features), f32),
                sem((9,)),
                sem((n_head,)),
                sem((n_sub - 1, n_head)),
                sem((n_sub - 1, n_head)),
                sem((heads, PIECES)),
                sem((heads, PIECES)),
                sem((n_sub - 1, heads)),
                sem((n_sub - 1, heads)),
                sem((n_head - 1, chunks)),
                sem((n_head - 1, chunks)),
            ],
            compiler_params=pltpu.CompilerParams(collective_id=0, has_side_effects=True),
            name="scoring",
        )
    ctx, opt = scoring(
        queries, keys, values, flat(opt_queries), flat(opt_keys), flat(opt_values),
        opt_offsets, opt_lengths, norm_gain.reshape(1, features), out_weight,
    )
    ctx, opt = pl.pallas_call(
        write_out,
        out_shape=(
            jax.ShapeDtypeStruct((rows, columns), bf16),
            jax.ShapeDtypeStruct((opts * slots, columns), bf16),
        ),
        in_specs=[anyspace, anyspace],
        out_specs=(anyspace, anyspace),
        scratch_shapes=[sem((2,))],
        compiler_params=pltpu.CompilerParams(vmem_limit_bytes=1 << 20),
        name="write_out",
    )(ctx, opt)
    return ctx, opt.reshape(opts, slots, columns)


def solution(mesh):
    placed = (
        P(("grp", "seq"), ("head", "sub")),
        P(("grp", "seq"), ("head", "sub")),
        P(("grp", "seq"), ("head", "sub")),
        P(("grp", "seq"), None, ("head", "sub")),
        P(("grp", "seq"), None, ("head", "sub")),
        P(("grp", "seq"), None, ("head", "sub")),
        P(("grp", "seq")),
        P(("grp", "seq")),
        P(("head", "sub")),
        P(("head", "sub"), None),
    )
    return jax.shard_map(
        on_device,
        mesh=mesh,
        in_specs=placed,
        out_specs=(P(("grp", "seq"), ("head", "sub")), P(("grp", "seq"), None, ("head", "sub"))),
        check_vma=False,
    )
```

```python
import functools

import jax
import jax.numpy as jnp
from jax import lax
from jax.experimental import pallas as pl
from jax.experimental.pallas import tpu as pltpu
from jax.sharding import PartitionSpec as P

DH = 128
PIECES = 2
PIECE = DH // PIECES
PARTS = 4
END = 384
WIDTH = 128
norm_epsilon = 1e-05
MESH = pl.DeviceIdType.MESH
bf16 = jnp.bfloat16
f32 = jnp.float32


def dot(a, b, ca, cb):
    return lax.dot_general(a, b, (((ca,), (cb,)), ((), ())), preferred_element_type=f32)


def kernel(
    sizes,
    q_hbm, k_hbm, v_hbm, oq_hbm, ok_hbm, ov_hbm, offs_hbm, lens_hbm, gain_hbm, w_hbm,
    ctx_out, opt_out,
    q_buf, k_buf, v_buf, state, intra, pre_recv, pre_send, normed, sib_normed,
    w_own, w_sib, part_send, part_recv, own_part,
    offs, lens, gain_ref,
    in_sem, w_sem, ws_send, ws_recv, pre_ssem, pre_rsem, n_send, n_recv, x_send, x_recv,
):
    n_seq, n_head, n_sub, rows, opts, slots, chunks = sizes
    features = q_hbm.shape[1]
    heads = features // DH
    total = rows + opts * slots
    columns = w_own.shape[2]
    width = columns // chunks
    seq = lax.axis_index("seq")
    head = lax.axis_index("head")
    sub = lax.axis_index("sub")

    barrier = pltpu.get_barrier_semaphore()
    for e in range(1, n_sub):
        pl.semaphore_signal(
            barrier, inc=1, device_id={"sub": lax.rem(sub + e, n_sub)}, device_id_type=MESH
        )
    for d in range(1, n_head):
        pl.semaphore_signal(
            barrier, inc=1, device_id={"head": lax.rem(head + d, n_head)}, device_id_type=MESH
        )

    @pl.when(seq > 0)
    def _():
        pl.semaphore_signal(barrier, inc=1, device_id={"seq": seq - 1}, device_id_type=MESH)

    @pl.when(seq < n_seq - 1)
    def _():
        pl.semaphore_signal(barrier, inc=1, device_id={"seq": seq + 1}, device_id_type=MESH)

    loads = []
    for i, (src, dst, at, count) in enumerate((
        (k_hbm, k_buf, 0, rows),
        (v_hbm, v_buf, 0, rows),
        (q_hbm, q_buf, 0, rows),
        (ok_hbm, k_buf, rows, opts * slots),
        (oq_hbm, q_buf, rows, opts * slots),
        (ov_hbm, v_buf, rows, opts * slots),
    )):
        copy = pltpu.make_async_copy(src, dst.at[pl.ds(at, count)], in_sem.at[i])
        copy.start()
        loads.append(copy)
    for i, (src, dst) in enumerate(((offs_hbm, offs), (lens_hbm, lens), (gain_hbm, gain_ref))):
        copy = pltpu.make_async_copy(src, dst, in_sem.at[6 + i])
        copy.start()
        loads.append(copy)

    def block_of(d, s):
        place = lax.rem(head + d, n_head) * n_sub + s
        return pl.ds(pl.multiple_of(place * columns, columns), columns)

    own_loads = []
    for d in range(n_head):
        copy = pltpu.make_async_copy(w_hbm.at[:, block_of(d, sub)], w_own.at[d], w_sem.at[d])
        own_loads.append(copy)

    def head_cols(h):
        return slice(h * DH, (h + 1) * DH)

    loads[0].wait()
    loads[1].wait()
    for h in range(heads):
        kh = k_buf[:rows, head_cols(h)].astype(bf16)
        vh = v_buf[:rows, head_cols(h)].astype(bf16)
        state[h] = dot(kh, vh, 0, 0)

    @pl.when(seq == 0)
    def _():
        for h in range(heads):
            pre_recv[h] = jnp.zeros((DH, DH), bf16)
            pre_send[h] = state[h].astype(bf16)

    greeted = (n_sub - 1) + (n_head - 1)
    around = jnp.where(seq > 0, 1, 0) + jnp.where(seq < n_seq - 1, 1, 0)
    pl.semaphore_wait(barrier, greeted + around)

    def pre_copy(h, p):
        return pltpu.make_async_remote_copy(
            src_ref=pre_send.at[h, pl.ds(p * PIECE, PIECE)],
            dst_ref=pre_recv.at[h, pl.ds(p * PIECE, PIECE)],
            send_sem=pre_ssem.at[h, p],
            recv_sem=pre_rsem.at[h, p],
            device_id={"seq": seq + 1},
            device_id_type=MESH,
        )

    @pl.when(jnp.logical_and(seq == 0, seq < n_seq - 1))
    def _():
        for h in range(heads):
            for p in range(PIECES):
                pre_copy(h, p).start()

    sib_copies = []
    for d in list(range(1, n_head)) + [0]:
        for e in range(1, n_sub):
            other = lax.rem(sub + e, n_sub)
            copy = pltpu.make_async_remote_copy(
                src_ref=w_hbm.at[:, block_of(d, other)],
                dst_ref=w_sib.at[e - 1, d],
                send_sem=ws_send.at[e - 1, d],
                recv_sem=ws_recv.at[e - 1, d],
                device_id={"sub": other},
                device_id_type=MESH,
            )
            copy.start()
            sib_copies.append(copy)
    for d in list(range(1, n_head)) + [0]:
        own_loads[d].start()

    for i in range(2, 9):
        loads[i].wait()

    ctx_mask = (
        lax.broadcasted_iota(jnp.int32, (rows, rows), 0)
        >= lax.broadcasted_iota(jnp.int32, (rows, rows), 1)
    )
    opt_masks = []
    for o in range(opts):
        col = lax.broadcasted_iota(jnp.int32, (slots, total), 1)
        row = lax.broadcasted_iota(jnp.int32, (slots, total), 0)
        first = rows + o * slots
        here = jnp.logical_and(col >= first, col <= row + first)
        opt_masks.append(jnp.logical_or(col < jnp.minimum(offs[o], rows), here))
    def relay(h):
        for p in range(PIECES):
            pre_copy(h, p).wait_recv()

            @pl.when(seq < n_seq - 1)
            def _():
                at = slice(p * PIECE, (p + 1) * PIECE)
                pre_send[h, at] = (state[h, at] + pre_recv[h, at].astype(f32)).astype(bf16)
                pre_copy(h, p).start()

    for h in range(heads):
        qh = q_buf[:, head_cols(h)].astype(bf16)
        kh = k_buf[:, head_cols(h)].astype(bf16)
        vh = v_buf[:, head_cols(h)].astype(bf16)
        scores = jnp.where(ctx_mask, dot(qh[:rows], kh[:rows], 1, 1), 0.0)
        intra[h, :rows] = dot(scores.astype(bf16), vh[:rows], 1, 0)
        opt_scores = dot(qh[rows:], kh, 1, 1)
        opt_scores = jnp.concatenate([
            jnp.where(opt_masks[o], opt_scores[o * slots:(o + 1) * slots], 0.0)
            for o in range(opts)
        ])
        intra[h, rows:] = dot(opt_scores.astype(bf16), vh, 1, 0)

        @pl.when(seq == 1)
        def _():
            relay(h)

    slot = lax.broadcasted_iota(jnp.int32, (slots, DH), 0)
    valid = [jnp.where(slot < lens[o], 1.0, 0.0) for o in range(opts)]

    n_copies = []
    for h in range(heads):
        @pl.when(seq > 1)
        def _():
            relay(h)

        qh = q_buf[:, head_cols(h)].astype(bf16)
        att = intra[h] + dot(qh, pre_recv[h], 1, 0)
        square = jnp.mean(att * att, axis=-1, keepdims=True)
        out = att * lax.rsqrt(square + norm_epsilon) * gain_ref[:, head_cols(h)]
        normed[:rows, head_cols(h)] = out[:rows].astype(bf16)
        for o in range(opts):
            at = slice(rows + o * slots, rows + (o + 1) * slots)
            normed[at, head_cols(h)] = (out[at] * valid[o]).astype(bf16)
        for e in range(1, n_sub):
            copy = pltpu.make_async_remote_copy(
                src_ref=normed.at[:, pl.ds(h * DH, DH)],
                dst_ref=sib_normed.at[e - 1, :, pl.ds(h * DH, DH)],
                send_sem=n_send.at[e - 1, h],
                recv_sem=n_recv.at[e - 1, h],
                device_id={"sub": lax.rem(sub + e, n_sub)},
                device_id_type=MESH,
            )
            copy.start()
            n_copies.append(copy)

    for d in range(n_head):
        own_loads[d].wait()
    for copy in sib_copies:
        copy.wait_recv()
    for copy in n_copies:
        copy.wait_recv()

    def project(d, c):
        at = pl.ds(c * width, width)
        result = dot(normed[...], w_own[d, :, at], 1, 0)
        for e in range(n_sub - 1):
            result = result + dot(sib_normed[e], w_sib[e, d, :, at], 1, 0)
        return result

    x_copies = {}
    for c in range(chunks):
        for d in range(1, n_head):
            part_send[d - 1, c] = project(d, c).astype(bf16)
            copy = pltpu.make_async_remote_copy(
                src_ref=part_send.at[d - 1, c],
                dst_ref=part_recv.at[d - 1, c],
                send_sem=x_send.at[d - 1, c],
                recv_sem=x_recv.at[d - 1, c],
                device_id={"head": lax.rem(head + d, n_head)},
                device_id_type=MESH,
            )
            copy.start()
            x_copies[d, c] = copy
    for c in range(chunks):
        own_part[c] = project(0, c)
    for c in range(chunks):
        result = own_part[c]
        for d in range(1, n_head):
            x_copies[d, c].wait_recv()
            result = result + part_recv[d - 1, c].astype(f32)
        at = slice(c * width, (c + 1) * width)
        ctx_out[:, at] = result[:rows].astype(bf16)
        opt_out[:, at] = result[rows:].astype(bf16)

    for copy in list(x_copies.values()) + n_copies + sib_copies:
        copy.wait_send()

    @pl.when(seq < n_seq - 1)
    def _():
        for h in range(heads):
            for p in range(PIECES):
                pre_copy(h, p).wait_send()


def shared_kernel(
    sizes,
    q_hbm, k_hbm, v_hbm, oq_hbm, ok_hbm, ov_hbm, offs_hbm, lens_hbm, gain_hbm, w_hbm,
    ctx_out, opt_out,
    q_buf, k_buf, v_buf, state, intra, pre_recv, pre_send, normed, sib_normed, far_normed,
    w_own, w_sib, w_own_end, w_sib_end, w_far, part_send, part_recv, acc,
    offs, lens, gain_ref,
    in_sem, w_sem, ws_send, ws_recv, pre_ssem, pre_rsem, n_send, n_recv,
    f_send, f_recv, r_send, r_recv, x_send, x_recv,
    wx_send, wf_recv, wy_send, wz_send, wd_send,
):
    n_seq, rows, opts, slots, near = sizes
    features = q_hbm.shape[1]
    heads = features // DH
    total = rows + opts * slots
    columns = w_own.shape[1]
    end = columns - near
    ends, width = part_send.shape[0], part_send.shape[2]
    parts = w_far.shape[2]
    band = DH // parts
    grp = lax.axis_index("grp")
    seq = lax.axis_index("seq")
    head = lax.axis_index("head")
    sub = lax.axis_index("sub")
    parity = lax.rem(seq, 2)
    mate = seq + 1 - 2 * parity
    sibling = {"sub": 1 - sub}
    across = {"head": 1 - head}
    beside = {"grp": 1 - grp}
    along = {"seq": mate}
    own_q = 2 * grp + parity
    y_q = 2 * (1 - grp) + parity
    z_q = 2 * grp + 1 - parity
    d_q = 2 * (1 - grp) + 1 - parity

    barrier = pltpu.get_barrier_semaphore()
    pl.semaphore_signal(barrier, inc=1, device_id=sibling, device_id_type=MESH)
    pl.semaphore_signal(barrier, inc=1, device_id=beside, device_id_type=MESH)
    for t in range(2):
        pl.semaphore_signal(
            barrier, inc=1, device_id={"head": 1 - head, "sub": t}, device_id_type=MESH
        )

    @pl.when(seq > 0)
    def _():
        pl.semaphore_signal(barrier, inc=1, device_id={"seq": seq - 1}, device_id_type=MESH)

    @pl.when(seq < n_seq - 1)
    def _():
        pl.semaphore_signal(barrier, inc=1, device_id={"seq": seq + 1}, device_id_type=MESH)

    loads = []
    for i, (src, dst, at, count) in enumerate((
        (k_hbm, k_buf, 0, rows),
        (v_hbm, v_buf, 0, rows),
        (q_hbm, q_buf, 0, rows),
        (ok_hbm, k_buf, rows, opts * slots),
        (oq_hbm, q_buf, rows, opts * slots),
        (ov_hbm, v_buf, rows, opts * slots),
    )):
        copy = pltpu.make_async_copy(src, dst.at[pl.ds(at, count)], in_sem.at[i])
        copy.start()
        loads.append(copy)
    for i, (src, dst) in enumerate(((offs_hbm, offs), (lens_hbm, lens), (gain_hbm, gain_ref))):
        copy = pltpu.make_async_copy(src, dst, in_sem.at[6 + i])
        copy.start()
        loads.append(copy)

    def block_of(h, s, start, count):
        return pl.ds(pl.multiple_of((h * 2 + s) * columns + start, 128), count)

    def remote(src, dst, send, recv, where):
        return pltpu.make_async_remote_copy(
            src_ref=src, dst_ref=dst, send_sem=send, recv_sem=recv,
            device_id=where, device_id_type=MESH,
        )

    def head_cols(h):
        return slice(h * DH, (h + 1) * DH)

    around = jnp.where(seq > 0, 1, 0) + jnp.where(seq < n_seq - 1, 1, 0)
    pl.semaphore_wait(barrier, 4 + around)

    wx_copies = []
    for i in range(parts):
        for t in range(2):
            at = pl.ds(pl.multiple_of(own_q * DH + i * band, band), band)
            copy = remote(
                w_hbm.at[at, block_of(1 - head, t, 0, near)], w_far.at[own_q, sub, i],
                wx_send.at[t, i], wf_recv.at[own_q, sub, i], {"head": 1 - head, "sub": t},
            )
            copy.start()
            wx_copies.append(copy)

    def arrived(q, s, i):
        piece = w_far.at[q, s, i]
        remote(piece, piece, wx_send.at[0, 0], wf_recv.at[q, s, i], across).wait_recv()

    def pass_on(q, s, i, send, where):
        piece = w_far.at[q, s, i]
        return remote(piece, piece, send, wf_recv.at[q, s, i], where)

    def y_copy(s, i):
        return pass_on(own_q, s, i, wy_send.at[s, i], beside)

    def z_copy(s, i):
        return pass_on(own_q, s, i, wz_send.at[s, i], along)

    def d_copy(s, i):
        if i % 2 == 0:
            return pass_on(y_q, s, i, wd_send.at[s, i], along)
        return pass_on(z_q, s, i, wd_send.at[s, i], beside)

    def own_event(i, y=True, z=True):
        for s in range(2):
            if y:
                arrived(own_q, s, i)
                y_copy(s, i).start()
            if z:
                z_copy(s, i).start()

    def next_event(i):
        for s in range(2):
            arrived(y_q, s, i)
            if i % 2 == 0:
                d_copy(s, i).start()
        for s in range(2):
            arrived(z_q, s, i)
            if i % 2 == 1:
                d_copy(s, i).start()

    loads[0].wait()
    loads[1].wait()
    for h in range(heads):
        kh = k_buf[:rows, head_cols(h)].astype(bf16)
        vh = v_buf[:rows, head_cols(h)].astype(bf16)
        state[h] = dot(kh, vh, 0, 0)

    def pre_copy(h, p):
        return remote(
            pre_send.at[h, pl.ds(p * PIECE, PIECE)], pre_recv.at[h, pl.ds(p * PIECE, PIECE)],
            pre_ssem.at[h, p], pre_rsem.at[h, p], {"seq": seq + 1},
        )

    @pl.when(seq == 0)
    def _():
        for h in range(heads):
            pre_recv[h] = jnp.zeros((DH, DH), bf16)
            pre_send[h] = state[h].astype(bf16)
        for h in range(heads):
            for p in range(PIECES):
                pre_copy(h, p).start()

    sib_copies = [
        remote(
            w_hbm.at[:, block_of(head, 1 - sub, 0, columns)], w_sib,
            ws_send.at[0], ws_recv.at[0], sibling,
        ),
        remote(
            w_hbm.at[:, block_of(1 - head, 1 - sub, near, end)], w_sib_end,
            ws_send.at[1], ws_recv.at[1], sibling,
        ),
    ]
    own_loads = [
        pltpu.make_async_copy(w_hbm.at[:, block_of(head, sub, 0, columns)], w_own, w_sem.at[0]),
        pltpu.make_async_copy(
            w_hbm.at[:, block_of(1 - head, sub, near, end)], w_own_end, w_sem.at[1]
        ),
    ]
    for copy in sib_copies + own_loads:
        copy.start()

    for i in range(2, 9):
        loads[i].wait()

    ctx_mask = (
        lax.broadcasted_iota(jnp.int32, (rows, rows), 0)
        >= lax.broadcasted_iota(jnp.int32, (rows, rows), 1)
    )
    opt_masks = []
    for o in range(opts):
        col = lax.broadcasted_iota(jnp.int32, (slots, total), 1)
        row = lax.broadcasted_iota(jnp.int32, (slots, total), 0)
        first = rows + o * slots
        here = jnp.logical_and(col >= first, col <= row + first)
        opt_masks.append(jnp.logical_or(col < jnp.minimum(offs[o], rows), here))

    def relay(h):
        for p in range(PIECES):
            pre_copy(h, p).wait_recv()

            @pl.when(seq < n_seq - 1)
            def _():
                at = slice(p * PIECE, (p + 1) * PIECE)
                pre_send[h, at] = (state[h, at] + pre_recv[h, at].astype(f32)).astype(bf16)
                pre_copy(h, p).start()

    for h in range(heads):
        qh = q_buf[:, head_cols(h)].astype(bf16)
        kh = k_buf[:, head_cols(h)].astype(bf16)
        vh = v_buf[:, head_cols(h)].astype(bf16)
        scores = jnp.where(ctx_mask, dot(qh[:rows], kh[:rows], 1, 1), 0.0)
        intra[h, :rows] = dot(scores.astype(bf16), vh[:rows], 1, 0)
        opt_scores = dot(qh[rows:], kh, 1, 1)
        opt_scores = jnp.concatenate([
            jnp.where(opt_masks[o], opt_scores[o * slots:(o + 1) * slots], 0.0)
            for o in range(opts)
        ])
        intra[h, rows:] = dot(opt_scores.astype(bf16), vh, 1, 0)


    slot = lax.broadcasted_iota(jnp.int32, (slots, DH), 0)
    valid = [jnp.where(slot < lens[o], 1.0, 0.0) for o in range(opts)]

    inner = jnp.logical_and(seq > 1, seq < n_seq - 1)

    @pl.when(inner)
    def _():
        own_event(0, z=False)

    @pl.when(seq == n_seq - 1)
    def _():
        own_event(0)

    @pl.when(seq > 2)
    def _():
        own_event(1)

    n_copies = []
    f_copies = []
    for h in range(heads):
        @pl.when(seq > 0)
        def _():
            relay(h)

        qh = q_buf[:, head_cols(h)].astype(bf16)
        att = intra[h] + dot(qh, pre_recv[h], 1, 0)
        square = jnp.mean(att * att, axis=-1, keepdims=True)
        out = att * lax.rsqrt(square + norm_epsilon) * gain_ref[:, head_cols(h)]
        normed[:rows, head_cols(h)] = out[:rows].astype(bf16)
        for o in range(opts):
            at = slice(rows + o * slots, rows + (o + 1) * slots)
            normed[at, head_cols(h)] = (out[at] * valid[o]).astype(bf16)
        place = pl.ds(pl.multiple_of(sub * DH, DH), DH)
        copy = remote(
            normed.at[:, pl.ds(h * DH, DH)], far_normed.at[h, :, place],
            f_send.at[h], f_recv.at[h], across,
        )
        copy.start()
        f_copies.append(copy)
        copy = remote(
            normed.at[:, pl.ds(h * DH, DH)], sib_normed.at[:, pl.ds(h * DH, DH)],
            n_send.at[h], n_recv.at[h], sibling,
        )
        copy.start()
        n_copies.append(copy)
        if h == 1:
            @pl.when(seq > 2)
            def _():
                own_event(2)

            @pl.when(inner)
            def _():
                own_event(1, z=False)

    @pl.when(inner)
    def _():
        own_event(0, y=False)

    @pl.when(seq < 2)
    def _():
        own_event(0)

    @pl.when(inner)
    def _():
        own_event(1, y=False)

    @pl.when(seq < 2)
    def _():
        own_event(1)

    r_copies = []
    x_copies = [
        remote(part_send.at[c], part_recv.at[c], x_send.at[c], x_recv.at[c], across)
        for c in range(ends)
    ]
    step = 256 if columns % 256 == 0 else columns

    def part():
        for copy in own_loads:
            copy.wait()
        for copy in sib_copies + n_copies:
            copy.wait_recv()
        for c in range(ends):
            at = slice(c * width, (c + 1) * width)
            result = dot(normed[...], w_own_end[:, at], 1, 0)
            result = result + dot(sib_normed[...], w_sib_end[:, at], 1, 0)
            part_send[c] = result.astype(bf16)
            x_copies[c].start()

    def keep(start):
        for c in range(start * step, columns, 2 * step):
            at = slice(c, c + step)
            acc[:, at] = (
                dot(normed[...], w_own[:, at], 1, 0) + dot(sib_normed[...], w_sib[:, at], 1, 0)
            )

    def hand_over(h):
        f_copies[h].wait_recv()
        piece = far_normed.at[h, :, place]
        copy = remote(piece, piece, r_send.at[h], r_recv.at[h], sibling)
        copy.start()
        r_copies.append(copy)

    @pl.when(seq < 3)
    def _():
        own_event(2)

    own_event(3)
    part()
    next_event(0)
    keep(0)
    next_event(1)
    keep(1)
    next_event(2)
    next_event(3)
    hand_over(0)
    hand_over(1)
    hand_over(2)
    hand_over(3)
    for i in range(parts):
        for s in range(2):
            arrived(d_q, s, i)
    other = pl.ds(pl.multiple_of((1 - sub) * DH, DH), DH)
    for h in range(heads):
        piece = far_normed.at[h, :, other]
        remote(piece, piece, r_send.at[h], r_recv.at[h], sibling).wait_recv()

    for c in range(0, near, step):
        at = slice(c, min(c + step, near))
        result = acc[:, at]
        for h in range(heads):
            weight = w_far[h, :, :, :, at].reshape(2 * DH, at.stop - at.start)
            result = result + dot(far_normed[h], weight, 1, 0)
        ctx_out[:, at] = result[:rows].astype(bf16)
        opt_out[:, at] = result[rows:].astype(bf16)
    for c in range(ends):
        x_copies[c].wait_recv()
        at = slice(near + c * width, near + (c + 1) * width)
        result = acc[:, at] + part_recv[c].astype(f32)
        ctx_out[:, at] = result[:rows].astype(bf16)
        opt_out[:, at] = result[rows:].astype(bf16)

    for copy in wx_copies + sib_copies + n_copies + f_copies + r_copies + x_copies:
        copy.wait_send()
    for s in range(2):
        for i in range(parts):
            y_copy(s, i).wait_send()
            z_copy(s, i).wait_send()
            d_copy(s, i).wait_send()

    @pl.when(seq < n_seq - 1)
    def _():
        for h in range(heads):
            for p in range(PIECES):
                pre_copy(h, p).wait_send()


def shared_call(n_seq, rows, opts, slots, features, columns):
    heads = features // DH
    total = rows + opts * slots
    near = columns - END
    sem = pltpu.SemaphoreType.DMA
    anyspace = pl.BlockSpec(memory_space=pl.ANY)
    vmem = pl.BlockSpec(memory_space=pltpu.VMEM)
    return pl.pallas_call(
        functools.partial(shared_kernel, (n_seq, rows, opts, slots, near)),
        out_shape=(
            pltpu.VMEM((rows, columns), bf16),
            pltpu.VMEM((opts * slots, columns), bf16),
        ),
        in_specs=[anyspace] * 10,
        out_specs=(vmem, vmem),
        scratch_shapes=[
            pltpu.VMEM((total, features), f32),
            pltpu.VMEM((total, features), f32),
            pltpu.VMEM((total, features), f32),
            pltpu.VMEM((heads, DH, DH), f32),
            pltpu.VMEM((heads, total, DH), f32),
            pltpu.VMEM((heads, DH, DH), bf16),
            pltpu.VMEM((heads, DH, DH), bf16),
            pltpu.VMEM((total, features), bf16),
            pltpu.VMEM((total, features), bf16),
            pltpu.VMEM((heads, total, 2 * DH), bf16),
            pltpu.VMEM((features, columns), bf16),
            pltpu.VMEM((features, columns), bf16),
            pltpu.VMEM((features, END), bf16),
            pltpu.VMEM((features, END), bf16),
            pltpu.VMEM((heads, 2, PARTS, DH // PARTS, near), bf16),
            pltpu.VMEM((END // WIDTH, total, WIDTH), bf16),
            pltpu.VMEM((END // WIDTH, total, WIDTH), bf16),
            pltpu.VMEM((total, columns), f32),
            pltpu.SMEM((opts,), jnp.int32),
            pltpu.SMEM((opts,), jnp.int32),
            pltpu.VMEM((1, features), f32),
            sem((9,)),
            sem((2,)),
            sem((2,)),
            sem((2,)),
            sem((heads, PIECES)),
            sem((heads, PIECES)),
            sem((heads,)),
            sem((heads,)),
            sem((heads,)),
            sem((heads,)),
            sem((heads,)),
            sem((heads,)),
            sem((END // WIDTH,)),
            sem((END // WIDTH,)),
            sem((2, PARTS)),
            sem((heads, 2, PARTS)),
            sem((2, PARTS)),
            sem((2, PARTS)),
            sem((2, PARTS)),
        ],
        compiler_params=pltpu.CompilerParams(collective_id=0, has_side_effects=True),
        name="scoring",
    )


def write_out(ctx, opt, ctx_hbm, opt_hbm, out_sem):
    copies = [
        pltpu.make_async_copy(ctx, ctx_hbm, out_sem.at[0]),
        pltpu.make_async_copy(opt, opt_hbm, out_sem.at[1]),
    ]
    for copy in copies:
        copy.start()
    for copy in copies:
        copy.wait()


def on_device(
    queries, keys, values, opt_queries, opt_keys, opt_values,
    opt_offsets, opt_lengths, norm_gain, out_weight,
):
    n_seq, n_head, n_sub = (lax.axis_size(a) for a in ("seq", "head", "sub"))
    rows, features = queries.shape
    opts, slots, _ = opt_queries.shape
    heads = features // DH
    total = rows + opts * slots
    columns = out_weight.shape[1] // (n_head * n_sub)
    width = 256 if columns % 256 == 0 else columns
    chunks = columns // width
    flat = lambda a: a.reshape(opts * slots, features)
    anyspace = pl.BlockSpec(memory_space=pl.ANY)
    vmem = pl.BlockSpec(memory_space=pltpu.VMEM)
    sem = pltpu.SemaphoreType.DMA
    shared = (
        lax.axis_size("grp") == 2 and n_head == 2 and n_sub == 2 and n_seq % 2 == 0
        and heads == 4 and columns > END
    )
    if shared:
        scoring = shared_call(n_seq, rows, opts, slots, features, columns)
    else:
        scoring = pl.pallas_call(
            functools.partial(kernel, (n_seq, n_head, n_sub, rows, opts, slots, chunks)),
            out_shape=(
                pltpu.VMEM((rows, columns), bf16),
                pltpu.VMEM((opts * slots, columns), bf16),
            ),
            in_specs=[anyspace] * 10,
            out_specs=(vmem, vmem),
            scratch_shapes=[
                pltpu.VMEM((total, features), f32),
                pltpu.VMEM((total, features), f32),
                pltpu.VMEM((total, features), f32),
                pltpu.VMEM((heads, DH, DH), f32),
                pltpu.VMEM((heads, total, DH), f32),
                pltpu.VMEM((heads, DH, DH), bf16),
                pltpu.VMEM((heads, DH, DH), bf16),
                pltpu.VMEM((total, features), bf16),
                pltpu.VMEM((n_sub - 1, total, features), bf16),
                pltpu.VMEM((n_head, features, columns), bf16),
                pltpu.VMEM((n_sub - 1, n_head, features, columns), bf16),
                pltpu.VMEM((n_head - 1, chunks, total, width), bf16),
                pltpu.VMEM((n_head - 1, chunks, total, width), bf16),
                pltpu.VMEM((chunks, total, width), f32),
                pltpu.SMEM((opts,), jnp.int32),
                pltpu.SMEM((opts,), jnp.int32),
                pltpu.VMEM((1, features), f32),
                sem((9,)),
                sem((n_head,)),
                sem((n_sub - 1, n_head)),
                sem((n_sub - 1, n_head)),
                sem((heads, PIECES)),
                sem((heads, PIECES)),
                sem((n_sub - 1, heads)),
                sem((n_sub - 1, heads)),
                sem((n_head - 1, chunks)),
                sem((n_head - 1, chunks)),
            ],
            compiler_params=pltpu.CompilerParams(collective_id=0, has_side_effects=True),
            name="scoring",
        )
    ctx, opt = scoring(
        queries, keys, values, flat(opt_queries), flat(opt_keys), flat(opt_values),
        opt_offsets, opt_lengths, norm_gain.reshape(1, features), out_weight,
    )
    ctx, opt = pl.pallas_call(
        write_out,
        out_shape=(
            jax.ShapeDtypeStruct((rows, columns), bf16),
            jax.ShapeDtypeStruct((opts * slots, columns), bf16),
        ),
        in_specs=[anyspace, anyspace],
        out_specs=(anyspace, anyspace),
        scratch_shapes=[sem((2,))],
        compiler_params=pltpu.CompilerParams(vmem_limit_bytes=1 << 20),
        name="write_out",
    )(ctx, opt)
    return ctx, opt.reshape(opts, slots, columns)


def solution(mesh):
    placed = (
        P(("grp", "seq"), ("head", "sub")),
        P(("grp", "seq"), ("head", "sub")),
        P(("grp", "seq"), ("head", "sub")),
        P(("grp", "seq"), None, ("head", "sub")),
        P(("grp", "seq"), None, ("head", "sub")),
        P(("grp", "seq"), None, ("head", "sub")),
        P(("grp", "seq")),
        P(("grp", "seq")),
        P(("head", "sub")),
        P(("head", "sub"), None),
    )
    return jax.shard_map(
        on_device,
        mesh=mesh,
        in_specs=placed,
        out_specs=(P(("grp", "seq"), ("head", "sub")), P(("grp", "seq"), None, ("head", "sub"))),
        check_vma=False,
    )
```

```python
import functools

import jax
import jax.numpy as jnp
from jax import lax
from jax.experimental import pallas as pl
from jax.experimental.pallas import tpu as pltpu
from jax.sharding import PartitionSpec as P

DH = 128
PIECES = 2
PIECE = DH // PIECES
PARTS = 4
END = 384
WIDTH = 128
norm_epsilon = 1e-05
MESH = pl.DeviceIdType.MESH
bf16 = jnp.bfloat16
f32 = jnp.float32


def dot(a, b, ca, cb):
    return lax.dot_general(a, b, (((ca,), (cb,)), ((), ())), preferred_element_type=f32)


def kernel(
    sizes,
    q_hbm, k_hbm, v_hbm, oq_hbm, ok_hbm, ov_hbm, offs_hbm, lens_hbm, gain_hbm, w_hbm,
    ctx_out, opt_out,
    q_buf, k_buf, v_buf, state, intra, pre_recv, pre_send, normed, sib_normed,
    w_own, w_sib, part_send, part_recv, own_part,
    offs, lens, gain_ref,
    in_sem, w_sem, ws_send, ws_recv, pre_ssem, pre_rsem, n_send, n_recv, x_send, x_recv,
):
    n_seq, n_head, n_sub, rows, opts, slots, chunks = sizes
    features = q_hbm.shape[1]
    heads = features // DH
    total = rows + opts * slots
    columns = w_own.shape[2]
    width = columns // chunks
    seq = lax.axis_index("seq")
    head = lax.axis_index("head")
    sub = lax.axis_index("sub")

    barrier = pltpu.get_barrier_semaphore()
    for e in range(1, n_sub):
        pl.semaphore_signal(
            barrier, inc=1, device_id={"sub": lax.rem(sub + e, n_sub)}, device_id_type=MESH
        )
    for d in range(1, n_head):
        pl.semaphore_signal(
            barrier, inc=1, device_id={"head": lax.rem(head + d, n_head)}, device_id_type=MESH
        )

    @pl.when(seq > 0)
    def _():
        pl.semaphore_signal(barrier, inc=1, device_id={"seq": seq - 1}, device_id_type=MESH)

    @pl.when(seq < n_seq - 1)
    def _():
        pl.semaphore_signal(barrier, inc=1, device_id={"seq": seq + 1}, device_id_type=MESH)

    loads = []
    for i, (src, dst, at, count) in enumerate((
        (k_hbm, k_buf, 0, rows),
        (v_hbm, v_buf, 0, rows),
        (q_hbm, q_buf, 0, rows),
        (ok_hbm, k_buf, rows, opts * slots),
        (oq_hbm, q_buf, rows, opts * slots),
        (ov_hbm, v_buf, rows, opts * slots),
    )):
        copy = pltpu.make_async_copy(src, dst.at[pl.ds(at, count)], in_sem.at[i])
        copy.start()
        loads.append(copy)
    for i, (src, dst) in enumerate(((offs_hbm, offs), (lens_hbm, lens), (gain_hbm, gain_ref))):
        copy = pltpu.make_async_copy(src, dst, in_sem.at[6 + i])
        copy.start()
        loads.append(copy)

    def block_of(d, s):
        place = lax.rem(head + d, n_head) * n_sub + s
        return pl.ds(pl.multiple_of(place * columns, columns), columns)

    own_loads = []
    for d in range(n_head):
        copy = pltpu.make_async_copy(w_hbm.at[:, block_of(d, sub)], w_own.at[d], w_sem.at[d])
        own_loads.append(copy)

    def head_cols(h):
        return slice(h * DH, (h + 1) * DH)

    loads[0].wait()
    loads[1].wait()
    for h in range(heads):
        kh = k_buf[:rows, head_cols(h)].astype(bf16)
        vh = v_buf[:rows, head_cols(h)].astype(bf16)
        state[h] = dot(kh, vh, 0, 0)

    @pl.when(seq == 0)
    def _():
        for h in range(heads):
            pre_recv[h] = jnp.zeros((DH, DH), bf16)
            pre_send[h] = state[h].astype(bf16)

    greeted = (n_sub - 1) + (n_head - 1)
    around = jnp.where(seq > 0, 1, 0) + jnp.where(seq < n_seq - 1, 1, 0)
    pl.semaphore_wait(barrier, greeted + around)

    def pre_copy(h, p):
        return pltpu.make_async_remote_copy(
            src_ref=pre_send.at[h, pl.ds(p * PIECE, PIECE)],
            dst_ref=pre_recv.at[h, pl.ds(p * PIECE, PIECE)],
            send_sem=pre_ssem.at[h, p],
            recv_sem=pre_rsem.at[h, p],
            device_id={"seq": seq + 1},
            device_id_type=MESH,
        )

    @pl.when(jnp.logical_and(seq == 0, seq < n_seq - 1))
    def _():
        for h in range(heads):
            for p in range(PIECES):
                pre_copy(h, p).start()

    sib_copies = []
    for d in list(range(1, n_head)) + [0]:
        for e in range(1, n_sub):
            other = lax.rem(sub + e, n_sub)
            copy = pltpu.make_async_remote_copy(
                src_ref=w_hbm.at[:, block_of(d, other)],
                dst_ref=w_sib.at[e - 1, d],
                send_sem=ws_send.at[e - 1, d],
                recv_sem=ws_recv.at[e - 1, d],
                device_id={"sub": other},
                device_id_type=MESH,
            )
            copy.start()
            sib_copies.append(copy)
    for d in list(range(1, n_head)) + [0]:
        own_loads[d].start()

    for i in range(2, 9):
        loads[i].wait()

    ctx_mask = (
        lax.broadcasted_iota(jnp.int32, (rows, rows), 0)
        >= lax.broadcasted_iota(jnp.int32, (rows, rows), 1)
    )
    opt_masks = []
    for o in range(opts):
        col = lax.broadcasted_iota(jnp.int32, (slots, total), 1)
        row = lax.broadcasted_iota(jnp.int32, (slots, total), 0)
        first = rows + o * slots
        here = jnp.logical_and(col >= first, col <= row + first)
        opt_masks.append(jnp.logical_or(col < jnp.minimum(offs[o], rows), here))
    def relay(h):
        for p in range(PIECES):
            pre_copy(h, p).wait_recv()

            @pl.when(seq < n_seq - 1)
            def _():
                at = slice(p * PIECE, (p + 1) * PIECE)
                pre_send[h, at] = (state[h, at] + pre_recv[h, at].astype(f32)).astype(bf16)
                pre_copy(h, p).start()

    for h in range(heads):
        qh = q_buf[:, head_cols(h)].astype(bf16)
        kh = k_buf[:, head_cols(h)].astype(bf16)
        vh = v_buf[:, head_cols(h)].astype(bf16)
        scores = jnp.where(ctx_mask, dot(qh[:rows], kh[:rows], 1, 1), 0.0)
        intra[h, :rows] = dot(scores.astype(bf16), vh[:rows], 1, 0)
        opt_scores = dot(qh[rows:], kh, 1, 1)
        opt_scores = jnp.concatenate([
            jnp.where(opt_masks[o], opt_scores[o * slots:(o + 1) * slots], 0.0)
            for o in range(opts)
        ])
        intra[h, rows:] = dot(opt_scores.astype(bf16), vh, 1, 0)

        @pl.when(seq == 1)
        def _():
            relay(h)

    slot = lax.broadcasted_iota(jnp.int32, (slots, DH), 0)
    valid = [jnp.where(slot < lens[o], 1.0, 0.0) for o in range(opts)]

    n_copies = []
    for h in range(heads):
        @pl.when(seq > 1)
        def _():
            relay(h)

        qh = q_buf[:, head_cols(h)].astype(bf16)
        att = intra[h] + dot(qh, pre_recv[h], 1, 0)
        square = jnp.mean(att * att, axis=-1, keepdims=True)
        out = att * lax.rsqrt(square + norm_epsilon) * gain_ref[:, head_cols(h)]
        normed[:rows, head_cols(h)] = out[:rows].astype(bf16)
        for o in range(opts):
            at = slice(rows + o * slots, rows + (o + 1) * slots)
            normed[at, head_cols(h)] = (out[at] * valid[o]).astype(bf16)
        for e in range(1, n_sub):
            copy = pltpu.make_async_remote_copy(
                src_ref=normed.at[:, pl.ds(h * DH, DH)],
                dst_ref=sib_normed.at[e - 1, :, pl.ds(h * DH, DH)],
                send_sem=n_send.at[e - 1, h],
                recv_sem=n_recv.at[e - 1, h],
                device_id={"sub": lax.rem(sub + e, n_sub)},
                device_id_type=MESH,
            )
            copy.start()
            n_copies.append(copy)

    for d in range(n_head):
        own_loads[d].wait()
    for copy in sib_copies:
        copy.wait_recv()
    for copy in n_copies:
        copy.wait_recv()

    def project(d, c):
        at = pl.ds(c * width, width)
        result = dot(normed[...], w_own[d, :, at], 1, 0)
        for e in range(n_sub - 1):
            result = result + dot(sib_normed[e], w_sib[e, d, :, at], 1, 0)
        return result

    x_copies = {}
    for c in range(chunks):
        for d in range(1, n_head):
            part_send[d - 1, c] = project(d, c).astype(bf16)
            copy = pltpu.make_async_remote_copy(
                src_ref=part_send.at[d - 1, c],
                dst_ref=part_recv.at[d - 1, c],
                send_sem=x_send.at[d - 1, c],
                recv_sem=x_recv.at[d - 1, c],
                device_id={"head": lax.rem(head + d, n_head)},
                device_id_type=MESH,
            )
            copy.start()
            x_copies[d, c] = copy
    for c in range(chunks):
        own_part[c] = project(0, c)
    for c in range(chunks):
        result = own_part[c]
        for d in range(1, n_head):
            x_copies[d, c].wait_recv()
            result = result + part_recv[d - 1, c].astype(f32)
        at = slice(c * width, (c + 1) * width)
        ctx_out[:, at] = result[:rows].astype(bf16)
        opt_out[:, at] = result[rows:].astype(bf16)

    for copy in list(x_copies.values()) + n_copies + sib_copies:
        copy.wait_send()

    @pl.when(seq < n_seq - 1)
    def _():
        for h in range(heads):
            for p in range(PIECES):
                pre_copy(h, p).wait_send()


def shared_kernel(
    sizes,
    q_hbm, k_hbm, v_hbm, oq_hbm, ok_hbm, ov_hbm, offs_hbm, lens_hbm, gain_hbm, w_hbm,
    ctx_out, opt_out,
    q_buf, k_buf, v_buf, state, intra, pre_recv, pre_send, normed, sib_normed, far_normed,
    w_own, w_sib, w_own_far, w_sib_far, w_far, part_send, part_recv, acc,
    offs, lens, gain_ref,
    in_sem, w_sem, ws_send, ws_recv, pre_ssem, pre_rsem, n_send, n_recv,
    f_send, f_recv, r_send, r_recv, x_send, x_recv,
    wx_send, wf_recv, wy_send, wz_send, wd_send,
):
    n_seq, rows, opts, slots, near = sizes
    features = q_hbm.shape[1]
    heads = features // DH
    total = rows + opts * slots
    columns = w_own.shape[1]
    width = part_send.shape[2]
    chunks, near_chunks = columns // width, near // width
    parts = w_far.shape[2]
    band = DH // parts
    grp = lax.axis_index("grp")
    seq = lax.axis_index("seq")
    head = lax.axis_index("head")
    sub = lax.axis_index("sub")
    parity = lax.rem(seq, 2)
    mate = seq + 1 - 2 * parity
    sibling = {"sub": 1 - sub}
    across = {"head": 1 - head}
    beside = {"grp": 1 - grp}
    along = {"seq": mate}
    own_q = 2 * grp + parity
    y_q = 2 * (1 - grp) + parity
    z_q = 2 * grp + 1 - parity
    d_q = 2 * (1 - grp) + 1 - parity

    late = seq > 1
    last = seq == n_seq - 1
    inner = jnp.logical_and(late, jnp.logical_not(last))
    early = jnp.logical_not(late)

    barrier = pltpu.get_barrier_semaphore()
    pl.semaphore_signal(barrier, inc=1, device_id=sibling, device_id_type=MESH)
    pl.semaphore_signal(barrier, inc=1, device_id=beside, device_id_type=MESH)
    for t in range(2):
        pl.semaphore_signal(
            barrier, inc=1, device_id={"head": 1 - head, "sub": t}, device_id_type=MESH
        )

    @pl.when(seq > 0)
    def _():
        pl.semaphore_signal(barrier, inc=1, device_id={"seq": seq - 1}, device_id_type=MESH)

    @pl.when(seq < n_seq - 1)
    def _():
        pl.semaphore_signal(barrier, inc=1, device_id={"seq": seq + 1}, device_id_type=MESH)

    loads = []
    for i, (src, dst, at, count) in enumerate((
        (k_hbm, k_buf, 0, rows),
        (v_hbm, v_buf, 0, rows),
        (q_hbm, q_buf, 0, rows),
        (ok_hbm, k_buf, rows, opts * slots),
        (oq_hbm, q_buf, rows, opts * slots),
        (ov_hbm, v_buf, rows, opts * slots),
    )):
        copy = pltpu.make_async_copy(src, dst.at[pl.ds(at, count)], in_sem.at[i])
        copy.start()
        loads.append(copy)
    for i, (src, dst) in enumerate(((offs_hbm, offs), (lens_hbm, lens), (gain_hbm, gain_ref))):
        copy = pltpu.make_async_copy(src, dst, in_sem.at[6 + i])
        copy.start()
        loads.append(copy)

    def block_of(h, s, start, count):
        return pl.ds(pl.multiple_of((h * 2 + s) * columns + start, 128), count)

    def remote(src, dst, send, recv, where):
        return pltpu.make_async_remote_copy(
            src_ref=src, dst_ref=dst, send_sem=send, recv_sem=recv,
            device_id=where, device_id_type=MESH,
        )

    def head_cols(h):
        return slice(h * DH, (h + 1) * DH)

    around = jnp.where(seq > 0, 1, 0) + jnp.where(seq < n_seq - 1, 1, 0)
    wx_copies = []
    for i in range(parts):
        for t in range(2):
            at = pl.ds(pl.multiple_of(own_q * DH + i * band, band), band)
            wx_copies.append(remote(
                w_hbm.at[at, block_of(1 - head, t, 0, near)], w_far.at[own_q, sub, i],
                wx_send.at[t, i], wf_recv.at[own_q, sub, i], {"head": 1 - head, "sub": t},
            ))

    sib_near = remote(
        w_hbm.at[:, block_of(1 - head, 1 - sub, 0, near)], w_sib_far.at[:, pl.ds(0, near)],
        ws_send.at[0], ws_recv.at[0], sibling,
    )
    sib_copies = [
        remote(
            w_hbm.at[:, block_of(1 - head, 1 - sub, near, columns - near)],
            w_sib_far.at[:, pl.ds(near, columns - near)],
            ws_send.at[1], ws_recv.at[1], sibling,
        ),
        remote(
            w_hbm.at[:, block_of(head, 1 - sub, 0, columns)], w_sib,
            ws_send.at[2], ws_recv.at[2], sibling,
        ),
    ]
    own_loads = [
        pltpu.make_async_copy(
            w_hbm.at[:, block_of(1 - head, sub, 0, columns)], w_own_far, w_sem.at[0]
        ),
        pltpu.make_async_copy(w_hbm.at[:, block_of(head, sub, 0, columns)], w_own, w_sem.at[1]),
    ]

    pl.semaphore_wait(barrier, 4 + around)

    @pl.when(late)
    def _():
        for copy in wx_copies:
            copy.start()

    @pl.when(early)
    def _():
        sib_near.start()

    sib_copies[0].start()
    own_loads[0].start()

    def arrived(q, s, i):
        piece = w_far.at[q, s, i]
        remote(piece, piece, wx_send.at[0, 0], wf_recv.at[q, s, i], across).wait_recv()

    def pass_on(q, s, i, send, where):
        piece = w_far.at[q, s, i]
        return remote(piece, piece, send, wf_recv.at[q, s, i], where)

    def y_copy(s, i):
        return pass_on(own_q, s, i, wy_send.at[s, i], beside)

    def z_copy(s, i):
        return pass_on(own_q, s, i, wz_send.at[s, i], along)

    def d_copy(s, i):
        if i % 2 == 0:
            return pass_on(y_q, s, i, wd_send.at[s, i], along)
        return pass_on(z_q, s, i, wd_send.at[s, i], beside)

    def own_event(i, y=True, z=True):
        for s in range(2):
            if y:
                arrived(own_q, s, i)
                y_copy(s, i).start()
            if z:
                z_copy(s, i).start()

    def next_event(i):
        for s in range(2):
            arrived(y_q, s, i)
            if i % 2 == 0:
                d_copy(s, i).start()
        for s in range(2):
            arrived(z_q, s, i)
            if i % 2 == 1:
                d_copy(s, i).start()

    loads[0].wait()
    loads[1].wait()
    for h in range(heads):
        kh = k_buf[:rows, head_cols(h)].astype(bf16)
        vh = v_buf[:rows, head_cols(h)].astype(bf16)
        state[h] = dot(kh, vh, 0, 0)

    def pre_copy(h, p):
        return remote(
            pre_send.at[h, pl.ds(p * PIECE, PIECE)], pre_recv.at[h, pl.ds(p * PIECE, PIECE)],
            pre_ssem.at[h, p], pre_rsem.at[h, p], {"seq": seq + 1},
        )

    @pl.when(seq == 0)
    def _():
        for h in range(heads):
            pre_recv[h] = jnp.zeros((DH, DH), bf16)
            pre_send[h] = state[h].astype(bf16)
        for h in range(heads):
            for p in range(PIECES):
                pre_copy(h, p).start()

    sib_copies[1].start()
    own_loads[1].start()

    for i in range(2, 9):
        loads[i].wait()

    ctx_mask = (
        lax.broadcasted_iota(jnp.int32, (rows, rows), 0)
        >= lax.broadcasted_iota(jnp.int32, (rows, rows), 1)
    )
    opt_masks = []
    for o in range(opts):
        col = lax.broadcasted_iota(jnp.int32, (slots, total), 1)
        row = lax.broadcasted_iota(jnp.int32, (slots, total), 0)
        first = rows + o * slots
        here = jnp.logical_and(col >= first, col <= row + first)
        opt_masks.append(jnp.logical_or(col < jnp.minimum(offs[o], rows), here))

    def relay(h):
        for p in range(PIECES):
            pre_copy(h, p).wait_recv()

            @pl.when(seq < n_seq - 1)
            def _():
                at = slice(p * PIECE, (p + 1) * PIECE)
                pre_send[h, at] = (state[h, at] + pre_recv[h, at].astype(f32)).astype(bf16)
                pre_copy(h, p).start()

    def inside_ctx(h):
        qh = q_buf[:rows, head_cols(h)].astype(bf16)
        kh = k_buf[:rows, head_cols(h)].astype(bf16)
        vh = v_buf[:rows, head_cols(h)].astype(bf16)
        scores = jnp.where(ctx_mask, dot(qh, kh, 1, 1), 0.0)
        intra[h, :rows] = dot(scores.astype(bf16), vh, 1, 0)

    def inside_opt(h):
        qh = q_buf[rows:, head_cols(h)].astype(bf16)
        kh = k_buf[:, head_cols(h)].astype(bf16)
        vh = v_buf[:, head_cols(h)].astype(bf16)
        opt_scores = dot(qh, kh, 1, 1)
        opt_scores = jnp.concatenate([
            jnp.where(opt_masks[o], opt_scores[o * slots:(o + 1) * slots], 0.0)
            for o in range(opts)
        ])
        intra[h, rows:] = dot(opt_scores.astype(bf16), vh, 1, 0)

    slot = lax.broadcasted_iota(jnp.int32, (slots, DH), 0)
    valid = [jnp.where(slot < lens[o], 1.0, 0.0) for o in range(opts)]

    spans = ((0, rows), (rows, opts * slots))

    def norm(h, kind):
        at = slice(spans[kind][0], spans[kind][0] + spans[kind][1])
        att = intra[h, at] + dot(q_buf[at, head_cols(h)].astype(bf16), pre_recv[h], 1, 0)
        square = jnp.mean(att * att, axis=-1, keepdims=True)
        out = att * lax.rsqrt(square + norm_epsilon) * gain_ref[:, head_cols(h)]
        if kind == 1:
            out = jnp.concatenate([
                out[o * slots:(o + 1) * slots] * valid[o] for o in range(opts)
            ])
        normed[at, head_cols(h)] = out.astype(bf16)

    def n_copy(h, kind):
        at = (pl.ds(*spans[kind]), pl.ds(h * DH, DH))
        return remote(
            normed.at[at], sib_normed.at[at], n_send.at[kind, h], n_recv.at[kind, h], sibling
        )

    @pl.when(seq == 0)
    def _():
        for kind, inside in enumerate((inside_ctx, inside_opt)):
            for h in range(heads):
                inside(h)
            for h in range(heads):
                norm(h, kind)
                n_copy(h, kind).start()

    @pl.when(seq > 0)
    def _():
        for h in range(heads):
            inside_ctx(h)
            inside_opt(h)

    @pl.when(inner)
    def _():
        own_event(0, z=False)

    @pl.when(last)
    def _():
        own_event(0)

    @pl.when(last)
    def _():
        own_event(1)

    place = pl.ds(pl.multiple_of(sub * DH, DH), DH)
    f_copies = [
        remote(
            normed.at[:, pl.ds(h * DH, DH)], far_normed.at[h, :, place],
            f_send.at[h], f_recv.at[h], across,
        )
        for h in range(heads)
    ]
    for h in range(heads):
        @pl.when(seq > 0)
        def _():
            relay(h)

        @pl.when(seq == 1)
        def _():
            norm(h, 0)
            n_copy(h, 0).start()

        @pl.when(late)
        def _():
            norm(h, 0)
            norm(h, 1)
            f_copies[h].start()
            for kind in range(2):
                n_copy(h, kind).start()

        if h == 1:
            @pl.when(last)
            def _():
                own_event(2)

            @pl.when(inner)
            def _():
                own_event(1, z=False)

    @pl.when(seq == 1)
    def _():
        for h in range(heads):
            norm(h, 1)
            n_copy(h, 1).start()

    def chunk(c, count=1):
        return slice(c * width, (c + count) * width)

    def x_copy(c, kind):
        at = pl.ds(*spans[kind])
        return remote(
            part_send.at[c, at], part_recv.at[c, at],
            x_send.at[kind, c], x_recv.at[kind, c], across,
        )

    def ready(kind):
        for h in range(heads):
            n_copy(h, kind).wait_recv()

    def loaded(i):
        own_loads[i].wait()
        sib_copies[i].wait_recv()

    def give(c, count, kind):
        at = chunk(c, count)
        lines = slice(spans[kind][0], spans[kind][0] + spans[kind][1])
        result = dot(normed[lines], w_own_far[:, at], 1, 0)
        result = result + dot(sib_normed[lines], w_sib_far[:, at], 1, 0)
        for k in range(count):
            part_send[c + k, lines] = result[:, chunk(k)].astype(bf16)
            x_copy(c + k, kind).start()

    def keep(c, count):
        at = chunk(c, count)
        acc[:, at] = dot(normed[...], w_own[:, at], 1, 0) + dot(sib_normed[...], w_sib[:, at], 1, 0)

    def put(at, result):
        ctx_out[:, at] = result[:rows].astype(bf16)
        opt_out[:, at] = result[rows:].astype(bf16)

    def take(c, kind):
        x_copy(c, kind).wait_recv()
        lines = slice(spans[kind][0], spans[kind][0] + spans[kind][1])
        result = acc[lines, chunk(c)] + part_recv[c, lines].astype(f32)
        (ctx_out, opt_out)[kind][:, chunk(c)] = result.astype(bf16)

    step = 256
    pair = step // width

    @pl.when(early)
    def _():
        loaded(0)
        sib_near.wait_recv()
        for kind in range(2):
            ready(kind)
            for c in range(0, chunks, pair):
                give(c, pair, kind)
        loaded(1)
        for c in range(0, chunks, pair):
            keep(c, pair)
        for kind in range(2):
            for c in range(chunks):
                take(c, kind)
        for kind in range(2):
            for c in range(chunks):
                x_copy(c, kind).wait_send()
        sib_near.wait_send()

    r_copies = []
    for h in range(heads):
        piece = far_normed.at[h, :, place]
        r_copies.append(remote(piece, piece, r_send.at[h], r_recv.at[h], sibling))

    @pl.when(late)
    def _():
        @pl.when(inner)
        def _():
            own_event(0, y=False)
            own_event(1, y=False)
            own_event(2)

        own_event(3)
        loaded(0)
        loaded(1)
        for kind in range(2):
            ready(kind)
        for c in range(near_chunks, chunks):
            for kind in range(2):
                give(c, 1, kind)
        next_event(0)
        for c in range(0, chunks, 2 * pair):
            keep(c, pair)
        next_event(1)
        for c in range(pair, chunks, 2 * pair):
            keep(c, pair)
        for i in range(2, parts):
            next_event(i)
        for h in range(heads):
            f_copies[h].wait_recv()
            r_copies[h].start()
        for i in range(parts):
            for s in range(2):
                arrived(d_q, s, i)
        other = pl.ds(pl.multiple_of((1 - sub) * DH, DH), DH)
        for h in range(heads):
            piece = far_normed.at[h, :, other]
            remote(piece, piece, r_send.at[h], r_recv.at[h], sibling).wait_recv()
        for c in range(0, near, step):
            at = slice(c, min(c + step, near))
            result = acc[:, at]
            for h in range(heads):
                weight = w_far[h, :, :, :, at].reshape(2 * DH, at.stop - at.start)
                result = result + dot(far_normed[h], weight, 1, 0)
            put(at, result)
        for c in range(near_chunks, chunks):
            for kind in range(2):
                take(c, kind)
                x_copy(c, kind).wait_send()
        for copy in wx_copies + f_copies + r_copies:
            copy.wait_send()
        for s in range(2):
            for i in range(parts):
                y_copy(s, i).wait_send()
                z_copy(s, i).wait_send()
                d_copy(s, i).wait_send()

    for copy in sib_copies:
        copy.wait_send()
    for kind in range(2):
        for h in range(heads):
            n_copy(h, kind).wait_send()

    @pl.when(seq < n_seq - 1)
    def _():
        for h in range(heads):
            for p in range(PIECES):
                pre_copy(h, p).wait_send()


def shared_call(n_seq, rows, opts, slots, features, columns):
    heads = features // DH
    total = rows + opts * slots
    near = columns - END
    sem = pltpu.SemaphoreType.DMA
    anyspace = pl.BlockSpec(memory_space=pl.ANY)
    vmem = pl.BlockSpec(memory_space=pltpu.VMEM)
    return pl.pallas_call(
        functools.partial(shared_kernel, (n_seq, rows, opts, slots, near)),
        out_shape=(
            pltpu.VMEM((rows, columns), bf16),
            pltpu.VMEM((opts * slots, columns), bf16),
        ),
        in_specs=[anyspace] * 10,
        out_specs=(vmem, vmem),
        scratch_shapes=[
            pltpu.VMEM((total, features), f32),
            pltpu.VMEM((total, features), f32),
            pltpu.VMEM((total, features), f32),
            pltpu.VMEM((heads, DH, DH), f32),
            pltpu.VMEM((heads, total, DH), f32),
            pltpu.VMEM((heads, DH, DH), bf16),
            pltpu.VMEM((heads, DH, DH), bf16),
            pltpu.VMEM((total, features), bf16),
            pltpu.VMEM((total, features), bf16),
            pltpu.VMEM((heads, total, 2 * DH), bf16),
            pltpu.VMEM((features, columns), bf16),
            pltpu.VMEM((features, columns), bf16),
            pltpu.VMEM((features, columns), bf16),
            pltpu.VMEM((features, columns), bf16),
            pltpu.VMEM((heads, 2, PARTS, DH // PARTS, near), bf16),
            pltpu.VMEM((columns // WIDTH, total, WIDTH), bf16),
            pltpu.VMEM((columns // WIDTH, total, WIDTH), bf16),
            pltpu.VMEM((total, columns), f32),
            pltpu.SMEM((opts,), jnp.int32),
            pltpu.SMEM((opts,), jnp.int32),
            pltpu.VMEM((1, features), f32),
            sem((9,)),
            sem((2,)),
            sem((3,)),
            sem((3,)),
            sem((heads, PIECES)),
            sem((heads, PIECES)),
            sem((2, heads)),
            sem((2, heads)),
            sem((heads,)),
            sem((heads,)),
            sem((heads,)),
            sem((heads,)),
            sem((2, columns // WIDTH)),
            sem((2, columns // WIDTH)),
            sem((2, PARTS)),
            sem((heads, 2, PARTS)),
            sem((2, PARTS)),
            sem((2, PARTS)),
            sem((2, PARTS)),
        ],
        compiler_params=pltpu.CompilerParams(collective_id=0, has_side_effects=True),
        name="scoring",
    )


def write_out(ctx, opt, ctx_hbm, opt_hbm, out_sem):
    copies = [
        pltpu.make_async_copy(ctx, ctx_hbm, out_sem.at[0]),
        pltpu.make_async_copy(opt, opt_hbm, out_sem.at[1]),
    ]
    for copy in copies:
        copy.start()
    for copy in copies:
        copy.wait()


def on_device(
    queries, keys, values, opt_queries, opt_keys, opt_values,
    opt_offsets, opt_lengths, norm_gain, out_weight,
):
    n_seq, n_head, n_sub = (lax.axis_size(a) for a in ("seq", "head", "sub"))
    rows, features = queries.shape
    opts, slots, _ = opt_queries.shape
    heads = features // DH
    total = rows + opts * slots
    columns = out_weight.shape[1] // (n_head * n_sub)
    width = 256 if columns % 256 == 0 else columns
    chunks = columns // width
    flat = lambda a: a.reshape(opts * slots, features)
    anyspace = pl.BlockSpec(memory_space=pl.ANY)
    vmem = pl.BlockSpec(memory_space=pltpu.VMEM)
    sem = pltpu.SemaphoreType.DMA
    shared = (
        lax.axis_size("grp") == 2 and n_head == 2 and n_sub == 2 and n_seq % 2 == 0
        and heads == 4 and columns > END and columns % 512 == 0
    )
    if shared:
        scoring = shared_call(n_seq, rows, opts, slots, features, columns)
    else:
        scoring = pl.pallas_call(
            functools.partial(kernel, (n_seq, n_head, n_sub, rows, opts, slots, chunks)),
            out_shape=(
                pltpu.VMEM((rows, columns), bf16),
                pltpu.VMEM((opts * slots, columns), bf16),
            ),
            in_specs=[anyspace] * 10,
            out_specs=(vmem, vmem),
            scratch_shapes=[
                pltpu.VMEM((total, features), f32),
                pltpu.VMEM((total, features), f32),
                pltpu.VMEM((total, features), f32),
                pltpu.VMEM((heads, DH, DH), f32),
                pltpu.VMEM((heads, total, DH), f32),
                pltpu.VMEM((heads, DH, DH), bf16),
                pltpu.VMEM((heads, DH, DH), bf16),
                pltpu.VMEM((total, features), bf16),
                pltpu.VMEM((n_sub - 1, total, features), bf16),
                pltpu.VMEM((n_head, features, columns), bf16),
                pltpu.VMEM((n_sub - 1, n_head, features, columns), bf16),
                pltpu.VMEM((n_head - 1, chunks, total, width), bf16),
                pltpu.VMEM((n_head - 1, chunks, total, width), bf16),
                pltpu.VMEM((chunks, total, width), f32),
                pltpu.SMEM((opts,), jnp.int32),
                pltpu.SMEM((opts,), jnp.int32),
                pltpu.VMEM((1, features), f32),
                sem((9,)),
                sem((n_head,)),
                sem((n_sub - 1, n_head)),
                sem((n_sub - 1, n_head)),
                sem((heads, PIECES)),
                sem((heads, PIECES)),
                sem((n_sub - 1, heads)),
                sem((n_sub - 1, heads)),
                sem((n_head - 1, chunks)),
                sem((n_head - 1, chunks)),
            ],
            compiler_params=pltpu.CompilerParams(collective_id=0, has_side_effects=True),
            name="scoring",
        )
    ctx, opt = scoring(
        queries, keys, values, flat(opt_queries), flat(opt_keys), flat(opt_values),
        opt_offsets, opt_lengths, norm_gain.reshape(1, features), out_weight,
    )
    ctx, opt = pl.pallas_call(
        write_out,
        out_shape=(
            jax.ShapeDtypeStruct((rows, columns), bf16),
            jax.ShapeDtypeStruct((opts * slots, columns), bf16),
        ),
        in_specs=[anyspace, anyspace],
        out_specs=(anyspace, anyspace),
        scratch_shapes=[sem((2,))],
        compiler_params=pltpu.CompilerParams(vmem_limit_bytes=1 << 20),
        name="write_out",
    )(ctx, opt)
    return ctx, opt.reshape(opts, slots, columns)


def solution(mesh):
    placed = (
        P(("grp", "seq"), ("head", "sub")),
        P(("grp", "seq"), ("head", "sub")),
        P(("grp", "seq"), ("head", "sub")),
        P(("grp", "seq"), None, ("head", "sub")),
        P(("grp", "seq"), None, ("head", "sub")),
        P(("grp", "seq"), None, ("head", "sub")),
        P(("grp", "seq")),
        P(("grp", "seq")),
        P(("head", "sub")),
        P(("head", "sub"), None),
    )
    return jax.shard_map(
        on_device,
        mesh=mesh,
        in_specs=placed,
        out_specs=(P(("grp", "seq"), ("head", "sub")), P(("grp", "seq"), None, ("head", "sub"))),
        check_vma=False,
    )
```
